32 devices in a mesh: bin: 4 (over x, core), frame: 8 (over z, y).
Axes of the slice: x: 2, y: 2, z: 4, core: 2. Of those that a mesh axis runs over, the one named last changes fastest.
Arguments:
- signal: bfloat16 [32, 2, 256, 2048], P('bin', None, None, 'frame'), may hold values from -24 to 24
- demix: float32 [32, 256, 512], P('bin'), may hold values from -1 to 2
Outputs:
- demixed: float32 [32, 256, 512], P('bin', 'frame')
- gradient: float32 [32, 256, 512], P('bin', 'frame')
The draws below stay inside these ranges and needn't reach their ends.
All inputs are finite; a program needn't handle non-finite values.
Results may differ from the reference program's by a relative error of at most 0.0061.
Values sent between devices are 32-bit elements; how exact they have to be, the bound alone decides.
A program may use at most 64 MiB of HBM per device.

```python
import math
import jax
import jax.numpy as jnp
from jax import lax

SENSOR_COUNT = 256
BINS = 32
ITERS = 2
TIME_FRAMES = 2048


def draw_signal(key, part):
    root_key, frequency_key, channel_key, pulse_key, frame_key = jax.random.split(jax.random.fold_in(key, 11), 5)
    shape = (BINS, 2, SENSOR_COUNT, TIME_FRAMES)
    root_seed = jnp.clip(jax.random.normal(root_key, shape, jnp.float32), -4.0, 4.0)
    frame_lo, frame_hi = (0.5, 2.0)
    bin_channel = jnp.exp(jax.random.uniform(frequency_key, (BINS, 1, SENSOR_COUNT, 1), jnp.float32, 0.0, math.log(3.0)))
    channel_scale = jnp.exp(jax.random.uniform(channel_key, (1, 1, SENSOR_COUNT, 1), jnp.float32, 0.0, math.log(2.0)))
    pulse_event = jnp.exp(jax.random.uniform(pulse_key, (1, 1, SENSOR_COUNT, TIME_FRAMES), jnp.float32, math.log(0.5), math.log(2.0)))
    frame_factor = jnp.exp(jax.random.uniform(frame_key, (1, 1, 1, TIME_FRAMES), jnp.float32, math.log(frame_lo), math.log(frame_hi)))
    return (0.25 * root_seed * bin_channel * channel_scale * pulse_event * frame_factor).astype(jnp.bfloat16)


def draw_demix(key, part):
    root_key = jax.random.fold_in(key, 23)
    shape = (BINS, SENSOR_COUNT, 2 * SENSOR_COUNT)
    root_seed = jnp.clip(jax.random.normal(root_key, shape, jnp.float32), -4.0, 4.0)
    row_ids = jnp.arange(SENSOR_COUNT).reshape(1, SENSOR_COUNT, 1)
    col_ids = jnp.arange(2 * SENSOR_COUNT).reshape(1, 1, 2 * SENSOR_COUNT)
    identity = jnp.where(row_ids == col_ids, 1.0, 0.0).astype(jnp.float32)
    return identity + 0.5 * root_seed / math.sqrt(SENSOR_COUNT)


def setup_inputs(seed: int = 0) -> dict:
    seeds = jax.random.split(jax.random.key(seed), 3)
    signal = draw_signal(jax.random.fold_in(seeds[2], 71), 0)
    demix = draw_demix(jax.random.fold_in(seeds[2], 71), 0)
    return dict(signal=signal, demix=demix)


step_size = 0.05
small_eps = 1e-06

def complex_matrix(demixing):
    width = demixing.shape[-1] // 2
    real_part = demixing[..., :width]
    imag_part = demixing[..., width:]
    upper = jnp.concatenate([real_part, imag_part], axis=-1)
    lower = jnp.concatenate([-imag_part, real_part], axis=-1)
    return jnp.concatenate([upper, lower], axis=-2)

def stack_signal(spectra):
    real_part = spectra[:, 0]
    imag_part = spectra[:, 1]
    upper = jnp.concatenate([real_part, imag_part], axis=-1)
    lower = jnp.concatenate([-imag_part, real_part], axis=-1)
    return jnp.concatenate([upper, lower], axis=-2)

def reference(signal, demix):
    frame_total = signal.shape[-1]
    demixing = demix
    direction = jnp.zeros_like(demix)
    for iteration in range(ITERS):
        rounded = demixing.astype(jnp.bfloat16)

        def one_bin(pair):
            weights, spectra = pair
            stacked = stack_signal(spectra[None])[0]
            return jnp.dot(weights, stacked, preferred_element_type=jnp.float32)
        sources = lax.map(one_bin, (rounded, signal))
        squares = lax.optimization_barrier(jnp.sum(sources * sources, axis=0))
        power_sum = squares[:, :frame_total] + squares[:, frame_total:]
        radius = jnp.sqrt(power_sum / BINS + small_eps)
        radius_both = jnp.concatenate([radius, radius], axis=1)

        def one_gram(values):
            scored = (values / radius_both).astype(jnp.bfloat16)
            source_b = values.astype(jnp.bfloat16)
            imag_key = jnp.concatenate([-source_b[:, frame_total:], source_b[:, :frame_total]], axis=1)
            dims = (((1,), (1,)), ((), ()))
            real_gram = lax.dot_general(scored, source_b, dims, preferred_element_type=jnp.float32)
            imag_gram = lax.dot_general(scored, imag_key, dims, preferred_element_type=jnp.float32)
            return jnp.concatenate([real_gram, imag_gram], axis=1) / frame_total
        gram_full = lax.map(one_gram, sources)
        product = jnp.einsum('fkj,fjl->fkl', gram_full, complex_matrix(demixing), precision=lax.Precision.HIGHEST)
        direction = demixing - product
        demixing = demixing + step_size * direction
    return (demixing, direction)
```

```python
import functools

import jax
import jax.numpy as jnp
from jax import lax
from jax.experimental import pallas as pl
from jax.experimental.pallas import tpu as pltpu
from jax.sharding import PartitionSpec as P

ITERS = 2
CHUNKS = 4
LAGS = (1, 3, 6)
EARLY = 3

step_size = 0.05
small_eps = 1e-06

MESH = pl.DeviceIdType.MESH
NT = (((1,), (1,)), ((), ()))
f32 = jnp.float32
bf16 = jnp.bfloat16


def dot(a, b):
    return jnp.dot(a, b, preferred_element_type=f32)


def dot_nt(a, b):
    return lax.dot_general(a, b, NT, preferred_element_type=f32)


def kernel(
    group, bin_group, sig, w_in, w_out, p_out,
    xs, xr, xb, tmp, flat, w_next, w_hi, w_lo, src, yb, gram, r1, part, r2a, r2b, own, prod,
    power, rinv, pa_r, pb_s, pb_r, pc_s, pc_r, pd_s, pd_r,
    x_send, x_recv, pw_send, pw_recv, s1a_send, s1a_recv, s2a_send, s2a_recv, g_send, g_recv,
    s1b_send, s1b_recv, s2b_send, s2b_recv, wx_send, wx_recv, dx_send, dx_recv,
):
    nb, high, _, _, rows, width2 = w_in.shape
    width = width2 // 2
    nt = sig.shape[3]
    nh = nb // 2
    total = 4 * high * rows
    half = total // 2
    quarter = total // 4
    eighth = total // 8
    chunk = half // CHUNKS
    frames = nt * group
    bins = nb * bin_group
    me = lax.axis_index("frame")
    mb = lax.axis_index("bin")
    y = lax.rem(me, 2)
    lo = lax.rem(me // 2, 2)
    hi = me // 4
    hib = hi // (high // 2)
    core = lax.rem(mb, 2)
    core_o = 1 - core
    y_dev = {"frame": me + 1 - 2 * y}
    lo_dev = {"frame": me + 2 - 4 * lo}
    core_dev = {"bin": mb + 1 - 2 * core}
    x_dev = {"bin": lax.rem(mb + 2, bin_group)}
    peers = [{"frame": lax.rem(hi + k, high) * 4 + lax.rem(me, 4)} for k in range(1, high)]

    def remote(a, b, s, r, dev):
        return pltpu.make_async_remote_copy(
            src_ref=a, dst_ref=b, send_sem=s, recv_sem=r, device_id=dev, device_id_type=MESH
        )

    def many(ref, sem):
        return pltpu.make_async_copy(ref, ref, sem)

    def x_copy(j, i):
        return remote(xs.at[j, i], xr.at[j, i], x_send.at[j, i], x_recv.at[j, i], lo_dev)

    def widen(j):
        xs[j] = sig[(1 - lo) * nh + j].astype(f32)

    barrier = pltpu.get_barrier_semaphore()
    for dev in [y_dev, lo_dev, core_dev, x_dev] + peers:
        pl.semaphore_signal(barrier, inc=1, device_id=dev, device_id_type=MESH)
    widen(0)
    pl.semaphore_wait(barrier, 4 + len(peers))
    x_copy(0, 0).start()
    x_copy(0, 1).start()
    widen(1)
    for n in range(2, EARLY):
        x_copy(n // 2, n % 2).start()

    def permute(f, to):
        for yd in range(2):
            for hd in range(high):
                for ld in range(2):
                    q = yd * 2 * high + hd * 2 + ld
                    to[q * rows:(q + 1) * rows, :] = w_in[f, hd, ld, yd]

    def times(wr, wi, xr_, xi_):
        return dot(wr, xr_) - dot(wi, xi_), dot(wr, xi_) + dot(wi, xr_)

    def keep(j, b, yr, yi):
        src[j, b, 0] = yr
        src[j, b, 1] = yi
        yb[j, b, 0] = yr.astype(bf16)
        yb[j, b, 1] = yi.astype(bf16)

    def split(j, w):
        big = w.astype(bf16)
        w_hi[j] = big
        w_lo[j] = (w - big.astype(f32)).astype(bf16)

    power[...] = jnp.zeros_like(power)

    def first(j, carry):
        f = lo * nh + j
        permute(f, flat.at[j])
        split(j, flat[j])
        yr, yi = times(w_hi[j, :, :width], w_hi[j, :, width:], sig[f, 0], sig[f, 1])
        keep(j, lo, yr, yi)
        power[0, lo] += yr * yr + yi * yi
        f = (1 - lo) * nh + j
        permute(f, tmp)
        wr, wi = tmp[:, :width].astype(bf16), tmp[:, width:].astype(bf16)
        yr, yi = times(wr, wi, sig[f, 0], sig[f, 1])
        power[0, lo] += yr * yr + yi * yi
        return carry

    lax.fori_loop(0, nh, first, 0)

    def half_of(k):
        return y if k % 2 else 1 - y

    def sub_of(k):
        return hib if k >= 2 else 1 - hib

    def piece(k, who):
        return pl.ds(pl.multiple_of(half_of(k) * half + sub_of(k) * quarter + who * eighth, eighth), eighth)

    def pw(it, k, step, block):
        sems = pw_send.at[it, k, step], pw_recv.at[it, k, step]
        if step == 0:
            if it == 0:
                return remote(power.at[0, block, piece(k, core_o)], pa_r.at[0, k, block], *sems, core_dev)
            return remote(power.at[1, :, piece(k, core_o)], pa_r.at[1, k], *sems, core_dev)
        if step == 3:
            return remote(pd_s.at[it, k], pd_r.at[it, k], *sems, core_dev)
        a, b, dev = (pb_s, pb_r, x_dev) if step == 1 else (pc_s, pc_r, lo_dev)
        if it == 0:
            return remote(a.at[0, k, block], b.at[0, k, block], *sems, dev)
        return remote(a.at[1, k], b.at[1, k], *sems, dev)

    def pw_a(it, k):
        pw(it, k, 0, lo).start()

    def pw_b(it, k):
        pw(it, k, 0, lo).wait()
        if it == 0:
            pb_s[0, k, lo] = power[0, lo, piece(k, core), :] + pa_r[0, k, lo]
        else:
            for b in range(2):
                pb_s[1, k, b] = power[1, b, piece(k, core), :] + pa_r[1, k, b]
        pw(it, k, 1, lo).start()

    def pw_c(it, k):
        pw(it, k, 1, lo).wait()
        if it == 0:
            pc_s[0, k, lo] = pb_s[0, k, lo] + pb_r[0, k, lo]
        else:
            pc_s[1, k] = pb_s[1, k] + pb_r[1, k]
        pw(it, k, 2, lo).start()

    def inverse(p):
        return 1.0 / jnp.sqrt(p / bins + small_eps)

    def pw_d(it, k):
        pw(it, k, 2, lo).wait_send()
        pw(it, k, 2, 1 - lo).wait_recv()
        if it == 0:
            pd_s[0, k, lo] = pc_s[0, k, lo]
            pd_s[0, k, 1 - lo] = pc_r[0, k, 1 - lo]
        else:
            pd_s[1, k] = pc_s[1, k] + pc_r[1, k]
        pw(it, k, 3, lo).start()
        for b in range(2):
            rinv[b, piece(k, core), :] = inverse(pd_s[it, k, b])

    def pw_e(it, k):
        pw(it, k, 3, lo).wait()
        for b in range(2):
            rinv[b, piece(k, core_o), :] = inverse(pd_r[it, k, b])

    for k in range(4):
        pw_a(0, k)
    for k in range(4):
        pw_b(0, k)
    for k in range(4):
        pw_c(0, k)
    for n in range(EARLY, 2 * nh):
        if n % 2 == 0:
            widen(n // 2)
        x_copy(n // 2, n % 2).start()
    for k in range(4):
        pw_d(0, k)
    for k in range(4):
        pw_e(0, k)

    def grams(j, its_rows):
        real = imag = None
        for b in range(2):
            inv = rinv[b, its_rows, :]
            pr = (src[j, b, 0, its_rows, :] * inv).astype(bf16)
            pi = (src[j, b, 1, its_rows, :] * inv).astype(bf16)
            br, bi = yb[j, b, 0], yb[j, b, 1]
            re = dot_nt(pr, br) + dot_nt(pi, bi)
            im = dot_nt(pi, br) - dot_nt(pr, bi)
            real, imag = (re, im) if b == 0 else (real + re, imag + im)
        return real, imag

    def triple(acc, j):
        n = acc.shape[0]
        both = jnp.concatenate([acc[:, :width], acc[:, width:]], axis=0)
        big = both.astype(bf16)
        small = (both - big.astype(f32)).astype(bf16)
        out = dot(big, w_hi[j]) + (dot(small, w_hi[j]) + dot(big, w_lo[j]))
        a, b = out[:n], out[n:]
        return a[:, :width] - b[:, width:], a[:, width:] + b[:, :width]

    def at(c):
        return pl.ds(pl.multiple_of(c * chunk, chunk), chunk)

    def at_own(c):
        return pl.ds(pl.multiple_of(y * half + c * chunk, chunk), chunk)

    def at_other(c):
        return pl.ds(pl.multiple_of((1 - y) * half + c * chunk, chunk), chunk)

    def s1a(j, c):
        return remote(gram.at[0, j, 1 - y, at(c)], r1.at[0, j, at(c)], s1a_send.at[j, c], s1a_recv.at[j, c], y_dev)

    def s2a(j, c, k):
        return remote(part.at[0, j, at(c)], r2a.at[j, c, k - 1], s2a_send.at[j, c], s2a_recv.at[j, c], peers[k - 1])

    def g(j, its_rows, c):
        ref = w_next.at[j, its_rows]
        return remote(ref, ref, g_send.at[j, c], g_recv.at[j, c], y_dev)

    def arrive(j):
        x_copy(j, 0).wait_recv()
        x_copy(j, 1).wait_recv()
        xb[j] = xr[j].astype(bf16)
        yr, yi = times(w_hi[j, :, :width], w_hi[j, :, width:], xb[j, 0], xb[j, 1])
        keep(j, 1 - lo, yr, yi)
        for away in range(2):
            h = y if away else 1 - y
            real, imag = grams(j, pl.ds(pl.multiple_of(h * half, half), half))
            gram[0, j, h, :, :width] = real
            gram[0, j, h, :, width:] = imag
            if away == 0:
                for c in range(CHUNKS):
                    s1a(j, c).start()

    def sum1(j, c):
        s1a(j, c).wait_recv()
        part[0, j, at(c)] = gram[0, j, y, at(c)] + r1[0, j, at(c)]
        for k in range(1, high):
            s2a(j, c, k).start()

    def update(j, c):
        many(r2a.at[j, c], s2a_recv.at[j, c]).wait()
        acc = part[0, j, at(c)]
        for k in range(high - 1):
            acc = acc + r2a[j, c, k]
        ar, ai = triple(acc * (1.0 / frames), j)
        w = flat[j, at_own(c)]
        wr, wi = w[:, :width], w[:, width:]
        w_next[j, at_own(c), :width] = wr + step_size * (wr - ar)
        w_next[j, at_own(c), width:] = wi + step_size * (wi - ai)
        g(j, at_own(c), c).start()

    def second(j):
        for c in range(CHUNKS):
            g(j, at_other(c), c).wait_recv()
        split(j, w_next[j])
        wr, wi = w_hi[j, :, :width], w_hi[j, :, width:]
        for b in range(2):
            yr, yi = times(wr, wi, *((sig[lo * nh + j, 0], sig[lo * nh + j, 1]) if b == 0 else (xb[j, 0], xb[j, 1])))
            block = lo if b == 0 else 1 - lo
            keep(j, block, yr, yi)
            power[1, block] += yr * yr + yi * yi

    units = nh * CHUNKS

    def pipeline(s, carry):
        def on(lag, stage):
            u = s - lag
            j, c = u // CHUNKS, lax.rem(u, CHUNKS)
            pl.when(jnp.logical_and(u >= 0, u < units))(lambda: stage(j, c))

        on(LAGS[0], sum1)
        on(LAGS[1], update)
        on(0, lambda j, c: pl.when(c == 0)(lambda: arrive(j)))
        on(LAGS[2], lambda j, c: pl.when(c == CHUNKS - 1)(lambda: second(j)))
        return carry

    lax.fori_loop(0, units + LAGS[2], pipeline, 0)

    far = [0, 1, 2, 3]
    for k in far:
        pw_a(1, k)

    def wx(j, from_lo):
        return remote(own.at[j, 1 - lo], w_out.at[from_lo * nh + j], wx_send.at[j], wx_recv.at[j], lo_dev)

    def dx(j, from_lo):
        return remote(prod.at[j, 1 - lo], p_out.at[from_lo * nh + j], dx_send.at[j], dx_recv.at[j], lo_dev)

    def s1b(j, i):
        sub = hib if i else 1 - hib
        its = pl.ds(pl.multiple_of(sub * quarter, quarter), quarter)
        return remote(gram.at[1, j, 1 - y, its], r1.at[1, j, its], s1b_send.at[j, i], s1b_recv.at[j, i], y_dev)

    def at_hi(h):
        return pl.ds(pl.multiple_of(h * 2 * rows, 2 * rows), 2 * rows)

    def s2b(j, k):
        return remote(
            part.at[1, j, at_hi(lax.rem(hi + k, high))], r2b.at[j, k - 1], s2b_send.at[j], s2b_recv.at[j], peers[k - 1]
        )

    def make_gram(k, j):
        h, sub = half_of(k), sub_of(k)
        real, imag = grams(j, pl.ds(pl.multiple_of(h * half + sub * quarter, quarter), quarter))
        its = pl.ds(pl.multiple_of(sub * quarter, quarter), quarter)
        gram[1, j, h, its, :width] = real
        gram[1, j, h, its, width:] = imag

    def sum1b(j, i):
        s1b(j, i).wait_recv()
        sub = hib if i else 1 - hib
        its = pl.ds(pl.multiple_of(sub * quarter, quarter), quarter)
        part[1, j, its] = gram[1, j, y, its] + r1[1, j, its]
        for k in range(1, high):
            target = lax.rem(hi + k, high)
            pl.when(target // (high // 2) == sub)(lambda k=k: s2b(j, k).start())

    def stage_k(k):
        def body(j, carry):
            make_gram(k, j)
            if k % 2 == 0:
                s1b(j, k // 2).start()
            return carry

        lax.fori_loop(0, nh, body, 0)

    for k in far:
        pw_b(1, k)
    pw_c(1, 0)
    pw_c(1, 1)
    pw_c(1, 2)
    pw_d(1, 0)
    pw_c(1, 3)
    pw_e(1, 0)
    stage_k(0)

    def mine(j, carry):
        start = pl.multiple_of(y * half + hi * 2 * rows, 2 * rows)
        w = w_next[j, pl.ds(start, 2 * rows), :]
        own[j, 0] = w[:rows]
        own[j, 1] = w[rows:]
        wx(j, lo).start()
        w_out[lo * nh + j] = own[j, lo]
        return carry

    lax.fori_loop(0, nh, mine, 0)
    pw_d(1, 1)
    pw_e(1, 1)
    stage_k(1)

    def loop_sum1b(i):
        def body(j, carry):
            sum1b(j, i)
            return carry

        lax.fori_loop(0, nh, body, 0)

    pw_d(1, 2)
    pw_e(1, 2)
    pw_d(1, 3)
    pw_e(1, 3)
    loop_sum1b(0)
    stage_k(2)
    stage_k(3)
    loop_sum1b(1)

    def finish(j, carry):
        many(r2b.at[j], s2b_recv.at[j]).wait()
        acc = part[1, j, at_hi(hi)]
        for k in range(high - 1):
            acc = acc + r2b[j, k]
        ar, ai = triple(acc * (1.0 / frames), j)
        for ld in range(2):
            prod[j, ld, :, :width] = ar[ld * rows:(ld + 1) * rows]
            prod[j, ld, :, width:] = ai[ld * rows:(ld + 1) * rows]
        dx(j, lo).start()
        p_out[lo * nh + j] = prod[j, lo]
        return carry

    lax.fori_loop(0, nh, finish, 0)

    def drain(j, carry):
        for i in range(2):
            x_copy(j, i).wait_send()
            s1b(j, i).wait_send()
        for c in range(CHUNKS):
            s1a(j, c).wait_send()
            many(r2a.at[j, c], s2a_send.at[j, c]).wait()
            g(j, at_own(c), c).wait_send()
        many(r2b.at[j], s2b_send.at[j]).wait()
        wx(j, lo).wait_send()
        wx(j, 1 - lo).wait_recv()
        dx(j, lo).wait_send()
        dx(j, 1 - lo).wait_recv()
        return carry

    lax.fori_loop(0, nh, drain, 0)


def on_device(signal, demix):
    group = lax.axis_size("frame")
    bin_group = lax.axis_size("bin")
    nb, _, sensors, nt = signal.shape
    total, width2 = demix.shape[1:]
    rows = total // group
    high = group // 4
    half = total // 2
    eighth = total // 8
    nh = nb // 2
    out = jax.ShapeDtypeStruct((nb, rows, width2), f32)
    dma = pltpu.SemaphoreType.DMA
    vmem = pl.BlockSpec(memory_space=pltpu.VMEM)
    piece = pltpu.VMEM((ITERS, 4, 2, eighth, nt), f32)
    own, product = pl.pallas_call(
        functools.partial(kernel, group, bin_group),
        out_shape=(out, out),
        in_specs=[vmem, vmem],
        out_specs=(vmem, vmem),
        scratch_shapes=[
            pltpu.VMEM((nh, 2, sensors, nt), f32),
            pltpu.VMEM((nh, 2, sensors, nt), f32),
            pltpu.VMEM((nh, 2, sensors, nt), bf16),
            pltpu.VMEM((total, width2), f32),
            pltpu.VMEM((nh, total, width2), f32),
            pltpu.VMEM((nh, total, width2), f32),
            pltpu.VMEM((nh, total, width2), bf16),
            pltpu.VMEM((nh, total, width2), bf16),
            pltpu.VMEM((nh, 2, 2, total, nt), f32),
            pltpu.VMEM((nh, 2, 2, total, nt), bf16),
            pltpu.VMEM((ITERS, nh, 2, half, width2), f32),
            pltpu.VMEM((ITERS, nh, half, width2), f32),
            pltpu.VMEM((ITERS, nh, half, width2), f32),
            pltpu.VMEM((nh, CHUNKS, high - 1, half // CHUNKS, width2), f32),
            pltpu.VMEM((nh, high - 1, 2 * rows, width2), f32),
            pltpu.VMEM((nh, 2, rows, width2), f32),
            pltpu.VMEM((nh, 2, rows, width2), f32),
            pltpu.VMEM((ITERS, 2, total, nt), f32),
            pltpu.VMEM((2, total, nt), f32),
            piece, piece, piece, piece, piece, piece, piece,
            dma((nh, 2)), dma((nh, 2)),
            dma((ITERS, 4, 4)), dma((ITERS, 4, 4)),
            dma((nh, CHUNKS)), dma((nh, CHUNKS)),
            dma((nh, CHUNKS)), dma((nh, CHUNKS)),
            dma((nh, CHUNKS)), dma((nh, CHUNKS)),
            dma((nh, 2)), dma((nh, 2)),
            dma((nh,)), dma((nh,)),
            dma((nh,)), dma((nh,)),
            dma((nh,)), dma((nh,)),
        ],
        compiler_params=pltpu.CompilerParams(
            collective_id=0, has_side_effects=True, vmem_limit_bytes=62 * 1024 * 1024
        ),
    )(signal, demix.reshape(nb, high, 2, 2, rows, width2))
    direction = own - product
    return own + step_size * direction, direction


def solution(mesh):
    placed = (P("bin", None, None, "frame"), P("bin", None, None))
    return jax.shard_map(
        on_device,
        mesh=mesh,
        in_specs=placed,
        out_specs=(P("bin", "frame", None), P("bin", "frame", None)),
        check_vma=False,
    )
```

```python
import functools

import jax
import jax.numpy as jnp
from jax import lax
from jax.experimental import pallas as pl
from jax.experimental.pallas import tpu as pltpu
from jax.sharding import PartitionSpec as P

ITERS = 2
CHUNKS = 4
LAGS = (1, 3, 6)
PIECES = 4
EARLY = 6
AHEAD = 8

step_size = 0.05
small_eps = 1e-06

MESH = pl.DeviceIdType.MESH
NT = (((1,), (1,)), ((), ()))
f32 = jnp.float32
bf16 = jnp.bfloat16


def dot(a, b):
    return jnp.dot(a, b, preferred_element_type=f32)


def dot_nt(a, b):
    return lax.dot_general(a, b, NT, preferred_element_type=f32)


def kernel(
    group, bin_group, sig, w_in, w_out, p_out,
    xs, xr, xb, tmp, flat, w_next, w_hi, w_lo, src, yb, gram, r1, part, last, r2a, r2b, own, prod,
    power, rinv, pa_r, pb_s, pb_r, pc_s, pc_r, pd_s, pd_r,
    x_send, x_recv, pw_send, pw_recv, s1a_send, s1a_recv, s2a_send, s2a_recv, g_send, g_recv,
    s1b_send, s1b_recv, s2b_send, s2b_recv, wx_send, wx_recv, dx_send, dx_recv,
):
    nb, high, _, _, rows, width2 = w_in.shape
    width = width2 // 2
    nt = sig.shape[3]
    nh = nb // 2
    total = 4 * high * rows
    half = total // 2
    quarter = total // 4
    eighth = total // 8
    chunk = half // CHUNKS
    frames = nt * group
    bins = nb * bin_group
    me = lax.axis_index("frame")
    mb = lax.axis_index("bin")
    y = lax.rem(me, 2)
    lo = lax.rem(me // 2, 2)
    hi = me // 4
    near = high // 2
    hib = hi // near
    hir = lax.rem(hi, near)
    core = lax.rem(mb, 2)
    core_o = 1 - core
    y_dev = {"frame": me + 1 - 2 * y}
    lo_dev = {"frame": me + 2 - 4 * lo}
    core_dev = {"bin": mb + 1 - 2 * core}
    x_dev = {"bin": lax.rem(mb + 2, bin_group)}
    peers = [{"frame": lax.rem(hi + k, high) * 4 + lax.rem(me, 4)} for k in range(1, high)]

    def remote(a, b, s, r, dev):
        return pltpu.make_async_remote_copy(
            src_ref=a, dst_ref=b, send_sem=s, recv_sem=r, device_id=dev, device_id_type=MESH
        )

    def many(ref, sem):
        return pltpu.make_async_copy(ref, ref, sem)

    def x_copy(j, p):
        deep = 2 * sig.shape[2] // PIECES
        ref = lambda a: a.at[j, p // 2, pl.ds(pl.multiple_of(lax.rem(p, 2) * deep, deep), deep)]
        return remote(ref(xs), ref(xr), x_send.at[j, p], x_recv.at[j, p], lo_dev)

    def widen(j):
        xs[j] = sig[(1 - lo) * nh + j].astype(f32)

    barrier = pltpu.get_barrier_semaphore()
    for dev in [y_dev, lo_dev, core_dev, x_dev] + peers:
        pl.semaphore_signal(barrier, inc=1, device_id=dev, device_id_type=MESH)
    widen(0)
    pl.semaphore_wait(barrier, 4 + len(peers))
    for n in range(EARLY):
        if n % PIECES == 0 and n > 0:
            widen(n // PIECES)
        x_copy(n // PIECES, n % PIECES).start()

    def permute(f, to):
        for yd in range(2):
            for hd in range(high):
                for ld in range(2):
                    q = yd * 2 * high + hd // near * 2 * near + ld * near + hd % near
                    to[q * rows:(q + 1) * rows, :] = w_in[f, hd, ld, yd]

    def times(wr, wi, xr_, xi_):
        return dot(wr, xr_) - dot(wi, xi_), dot(wr, xi_) + dot(wi, xr_)

    def keep(j, b, yr, yi):
        src[j, b, 0] = yr
        src[j, b, 1] = yi
        yb[j, b, 0] = yr.astype(bf16)
        yb[j, b, 1] = yi.astype(bf16)

    def split(j, w):
        big = w.astype(bf16)
        w_hi[j] = big
        w_lo[j] = (w - big.astype(f32)).astype(bf16)

    power[...] = jnp.zeros_like(power)

    def first(j, carry):
        f = lo * nh + j
        permute(f, flat.at[j])
        split(j, flat[j])
        yr, yi = times(w_hi[j, :, :width], w_hi[j, :, width:], sig[f, 0], sig[f, 1])
        keep(j, lo, yr, yi)
        power[0, lo] += yr * yr + yi * yi
        f = (1 - lo) * nh + j
        permute(f, tmp)
        wr, wi = tmp[:, :width].astype(bf16), tmp[:, width:].astype(bf16)
        yr, yi = times(wr, wi, sig[f, 0], sig[f, 1])
        power[0, lo] += yr * yr + yi * yi
        return carry

    lax.fori_loop(0, nh, first, 0)

    def half_of(k):
        return y if k % 2 else 1 - y

    def sub_of(k):
        return hib if k >= 2 else 1 - hib

    def piece(k, who):
        return pl.ds(pl.multiple_of(half_of(k) * half + sub_of(k) * quarter + who * eighth, eighth), eighth)

    def pw(it, k, step, block):
        sems = pw_send.at[it, k, step], pw_recv.at[it, k, step]
        if step == 0:
            if it == 0:
                return remote(power.at[0, block, piece(k, core_o)], pa_r.at[0, k, block], *sems, core_dev)
            return remote(power.at[1, :, piece(k, core_o)], pa_r.at[1, k], *sems, core_dev)
        if step == 3:
            return remote(pd_s.at[it, k], pd_r.at[it, k], *sems, core_dev)
        a, b, dev = (pb_s, pb_r, x_dev) if step == 1 else (pc_s, pc_r, lo_dev)
        if it == 0:
            return remote(a.at[0, k, block], b.at[0, k, block], *sems, dev)
        return remote(a.at[1, k], b.at[1, k], *sems, dev)

    def pw_a(it, k):
        pw(it, k, 0, lo).start()

    def pw_b(it, k):
        pw(it, k, 0, lo).wait()
        if it == 0:
            pb_s[0, k, lo] = power[0, lo, piece(k, core), :] + pa_r[0, k, lo]
        else:
            for b in range(2):
                pb_s[1, k, b] = power[1, b, piece(k, core), :] + pa_r[1, k, b]
        pw(it, k, 1, lo).start()

    def pw_c(it, k):
        pw(it, k, 1, lo).wait()
        if it == 0:
            pc_s[0, k, lo] = pb_s[0, k, lo] + pb_r[0, k, lo]
        else:
            pc_s[1, k] = pb_s[1, k] + pb_r[1, k]
        pw(it, k, 2, lo).start()

    def inverse(p):
        return 1.0 / jnp.sqrt(p / bins + small_eps)

    def pw_d(it, k):
        pw(it, k, 2, lo).wait_send()
        pw(it, k, 2, 1 - lo).wait_recv()
        if it == 0:
            pd_s[0, k, lo] = pc_s[0, k, lo]
            pd_s[0, k, 1 - lo] = pc_r[0, k, 1 - lo]
        else:
            pd_s[1, k] = pc_s[1, k] + pc_r[1, k]
        pw(it, k, 3, lo).start()
        for b in range(2):
            rinv[b, piece(k, core), :] = inverse(pd_s[it, k, b])

    def pw_e(it, k):
        pw(it, k, 3, lo).wait()
        for b in range(2):
            rinv[b, piece(k, core_o), :] = inverse(pd_r[it, k, b])

    for k in range(4):
        pw_a(0, k)
    for k in range(4):
        pw_b(0, k)
    for k in range(4):
        pw_c(0, k)
    for j in range((EARLY + PIECES - 1) // PIECES, nh):
        widen(j)
    for n in range(EARLY, AHEAD):
        x_copy(n // PIECES, n % PIECES).start()
    for k in range(4):
        pw_d(0, k)
    for k in range(4):
        pw_e(0, k)

    def grams(j, its_rows):
        real = imag = None
        for b in range(2):
            inv = rinv[b, its_rows, :]
            pr = (src[j, b, 0, its_rows, :] * inv).astype(bf16)
            pi = (src[j, b, 1, its_rows, :] * inv).astype(bf16)
            br, bi = yb[j, b, 0], yb[j, b, 1]
            re = dot_nt(pr, br) + dot_nt(pi, bi)
            im = dot_nt(pi, br) - dot_nt(pr, bi)
            real, imag = (re, im) if b == 0 else (real + re, imag + im)
        return real, imag

    def triple(acc, j):
        n = acc.shape[0]
        both = jnp.concatenate([acc[:, :width], acc[:, width:]], axis=0)
        big = both.astype(bf16)
        small = (both - big.astype(f32)).astype(bf16)
        out = dot(big, w_hi[j]) + (dot(small, w_hi[j]) + dot(big, w_lo[j]))
        a, b = out[:n], out[n:]
        return a[:, :width] - b[:, width:], a[:, width:] + b[:, :width]

    def at(c):
        return pl.ds(pl.multiple_of(c * chunk, chunk), chunk)

    def at_own(c):
        return pl.ds(pl.multiple_of(y * half + c * chunk, chunk), chunk)

    def at_other(c):
        return pl.ds(pl.multiple_of((1 - y) * half + c * chunk, chunk), chunk)

    def s1a(j, c):
        return remote(gram.at[0, j, 1 - y, at(c)], r1.at[0, j, at(c)], s1a_send.at[j, c], s1a_recv.at[j, c], y_dev)

    def s2a(j, c, k):
        return remote(part.at[j, at(c)], r2a.at[j, c, k - 1], s2a_send.at[j, c], s2a_recv.at[j, c], peers[k - 1])

    def g(j, its_rows, c):
        ref = w_next.at[j, its_rows]
        return remote(ref, ref, g_send.at[j, c], g_recv.at[j, c], y_dev)

    def arrive(j):
        for p in range(PIECES):
            x_copy(j, p).wait_recv()
        xb[j] = xr[j].astype(bf16)
        yr, yi = times(w_hi[j, :, :width], w_hi[j, :, width:], xb[j, 0], xb[j, 1])
        keep(j, 1 - lo, yr, yi)
        for away in range(2):
            h = y if away else 1 - y
            real, imag = grams(j, pl.ds(pl.multiple_of(h * half, half), half))
            gram[0, j, h, :, :width] = real
            gram[0, j, h, :, width:] = imag
            if away == 0:
                for c in range(CHUNKS):
                    s1a(j, c).start()

    def sum1(j, c):
        s1a(j, c).wait_recv()
        part[j, at(c)] = gram[0, j, y, at(c)] + r1[0, j, at(c)]
        for k in range(1, high):
            s2a(j, c, k).start()
        n = j * CHUNKS + c + AHEAD
        pl.when(n < nh * PIECES)(lambda: x_copy(n // PIECES, lax.rem(n, PIECES)).start())

    def update(j, c):
        many(r2a.at[j, c], s2a_recv.at[j, c]).wait()
        acc = part[j, at(c)]
        for k in range(high - 1):
            acc = acc + r2a[j, c, k]
        ar, ai = triple(acc * (1.0 / frames), j)
        w = flat[j, at_own(c)]
        wr, wi = w[:, :width], w[:, width:]
        w_next[j, at_own(c), :width] = wr + step_size * (wr - ar)
        w_next[j, at_own(c), width:] = wi + step_size * (wi - ai)
        g(j, at_own(c), c).start()

    def second(j):
        for c in range(CHUNKS):
            g(j, at_other(c), c).wait_recv()
        split(j, w_next[j])
        wr, wi = w_hi[j, :, :width], w_hi[j, :, width:]
        for b in range(2):
            yr, yi = times(wr, wi, *((sig[lo * nh + j, 0], sig[lo * nh + j, 1]) if b == 0 else (xb[j, 0], xb[j, 1])))
            block = lo if b == 0 else 1 - lo
            keep(j, block, yr, yi)
            power[1, block] += yr * yr + yi * yi

    units = nh * CHUNKS

    def pipeline(s, carry):
        def on(lag, stage):
            u = s - lag
            j, c = u // CHUNKS, lax.rem(u, CHUNKS)
            pl.when(jnp.logical_and(u >= 0, u < units))(lambda: stage(j, c))

        on(LAGS[0], sum1)
        on(LAGS[1], update)
        on(0, lambda j, c: pl.when(c == 0)(lambda: arrive(j)))
        on(LAGS[2], lambda j, c: pl.when(c == CHUNKS - 1)(lambda: second(j)))
        return carry

    lax.fori_loop(0, units + LAGS[2], pipeline, 0)

    for k in range(4):
        pw_a(1, k)

    def wx(j, from_lo):
        return remote(own.at[j, 1 - lo], w_out.at[from_lo * nh + j], wx_send.at[j], wx_recv.at[j], lo_dev)

    def dx(j, from_lo):
        return remote(prod.at[j], p_out.at[from_lo * nh + j], dx_send.at[j], dx_recv.at[j], lo_dev)

    def at_piece(i, l):
        sub = hib if i else 1 - hib
        side = lo if l else 1 - lo
        return pl.ds(pl.multiple_of(sub * quarter + side * eighth, eighth), eighth)

    def s1b(j, i, l):
        its = at_piece(i, l)
        return remote(gram.at[1, j, 1 - y, its], r1.at[1, j, its], s1b_send.at[j, i, l], s1b_recv.at[j, i, l], y_dev)

    def s2b(j, l, k):
        target = lax.rem(hi + k, high)
        return remote(
            last.at[j, l, target], r2b.at[j, l, k - 1], s2b_send.at[j, l], s2b_recv.at[j, l], peers[k - 1]
        )

    def make_gram(k, j):
        h, sub = half_of(k), sub_of(k)
        real, imag = grams(j, pl.ds(pl.multiple_of(h * half + sub * quarter, quarter), quarter))
        its = pl.ds(pl.multiple_of(sub * quarter, quarter), quarter)
        gram[1, j, h, its, :width] = real
        gram[1, j, h, its, width:] = imag

    def sum1b(j, i, l):
        s1b(j, i, l).wait_recv()
        its = at_piece(i, l)
        value = gram[1, j, y, its] + r1[1, j, its]
        sub = hib if i else 1 - hib
        for r in range(near):
            last[j, l, sub * near + r] = value[r * rows:(r + 1) * rows]
        for k in range(1, high):
            there = lax.rem(hi + k, high) // near == sub
            pl.when(there)(lambda k=k: s2b(j, l, k).start())

    def each(stage):
        def body(j, carry):
            stage(j)
            return carry

        lax.fori_loop(0, nh, body, 0)

    for k in range(4):
        pw_b(1, k)
    pw_c(1, 0)
    pw_c(1, 1)
    pw_c(1, 2)
    pw_d(1, 0)
    pw_c(1, 3)
    pw_e(1, 0)

    def gram_away(k, j):
        make_gram(k, j)
        s1b(j, k // 2, 0).start()

    each(functools.partial(gram_away, 0))
    each(lambda j: s1b(j, 0, 1).start())
    pw_d(1, 1)
    pw_e(1, 1)
    each(functools.partial(make_gram, 1))
    pw_d(1, 2)
    pw_e(1, 2)
    each(lambda j: sum1b(j, 0, 0))
    each(functools.partial(gram_away, 2))
    each(lambda j: s1b(j, 1, 1).start())
    pw_d(1, 3)
    pw_e(1, 3)

    def mine(j):
        start = pl.multiple_of(y * half + hib * quarter, quarter)
        w = w_next[j, pl.ds(start, quarter), :]
        for l in range(2):
            for r in range(near):
                q = l * near + r
                if near == 1:
                    own[j, l] = w[q * rows:(q + 1) * rows]
                else:
                    pl.when(hir == r)(functools.partial(place, j, l, w[q * rows:(q + 1) * rows]))
        wx(j, lo).start()
        w_out[lo * nh + j] = own[j, lo]

    def place(j, l, w):
        own[j, l] = w

    each(lambda j: sum1b(j, 0, 1))
    each(functools.partial(make_gram, 3))
    each(mine)

    def finish(j, l):
        many(r2b.at[j, l], s2b_recv.at[j, l]).wait()
        acc = last[j, l, hi]
        for k in range(high - 1):
            acc = acc + r2b[j, l, k]
        ar, ai = triple(acc * (1.0 / frames), j)
        if l == 0:
            prod[j, :, :width] = ar
            prod[j, :, width:] = ai
            dx(j, lo).start()
        else:
            p_out[lo * nh + j, :, :width] = ar
            p_out[lo * nh + j, :, width:] = ai

    def close(l):
        def body(j):
            sum1b(j, 1, l)
            finish(j, l)

        each(body)

    close(0)
    close(1)

    def drain(j):
        for p in range(PIECES):
            x_copy(j, p).wait_send()
        for c in range(CHUNKS):
            s1a(j, c).wait_send()
            many(r2a.at[j, c], s2a_send.at[j, c]).wait()
            g(j, at_own(c), c).wait_send()
        for l in range(2):
            for i in range(2):
                s1b(j, i, l).wait_send()
            many(r2b.at[j, l], s2b_send.at[j, l]).wait()
        wx(j, lo).wait_send()
        wx(j, 1 - lo).wait_recv()
        dx(j, lo).wait_send()
        dx(j, 1 - lo).wait_recv()

    each(drain)


def on_device(signal, demix):
    group = lax.axis_size("frame")
    bin_group = lax.axis_size("bin")
    nb, _, sensors, nt = signal.shape
    total, width2 = demix.shape[1:]
    rows = total // group
    high = group // 4
    half = total // 2
    eighth = total // 8
    nh = nb // 2
    out = jax.ShapeDtypeStruct((nb, rows, width2), f32)
    dma = pltpu.SemaphoreType.DMA
    vmem = pl.BlockSpec(memory_space=pltpu.VMEM)
    piece = pltpu.VMEM((ITERS, 4, 2, eighth, nt), f32)
    own, product = pl.pallas_call(
        functools.partial(kernel, group, bin_group),
        out_shape=(out, out),
        in_specs=[vmem, vmem],
        out_specs=(vmem, vmem),
        scratch_shapes=[
            pltpu.VMEM((nh, 2, sensors, nt), f32),
            pltpu.VMEM((nh, 2, sensors, nt), f32),
            pltpu.VMEM((nh, 2, sensors, nt), bf16),
            pltpu.VMEM((total, width2), f32),
            pltpu.VMEM((nh, total, width2), f32),
            pltpu.VMEM((nh, total, width2), f32),
            pltpu.VMEM((nh, total, width2), bf16),
            pltpu.VMEM((nh, total, width2), bf16),
            pltpu.VMEM((nh, 2, 2, total, nt), f32),
            pltpu.VMEM((nh, 2, 2, total, nt), bf16),
            pltpu.VMEM((ITERS, nh, 2, half, width2), f32),
            pltpu.VMEM((ITERS, nh, half, width2), f32),
            pltpu.VMEM((nh, half, width2), f32),
            pltpu.VMEM((nh, 2, high, rows, width2), f32),
            pltpu.VMEM((nh, CHUNKS, high - 1, half // CHUNKS, width2), f32),
            pltpu.VMEM((nh, 2, high - 1, rows, width2), f32),
            pltpu.VMEM((nh, 2, rows, width2), f32),
            pltpu.VMEM((nh, rows, width2), f32),
            pltpu.VMEM((ITERS, 2, total, nt), f32),
            pltpu.VMEM((2, total, nt), f32),
            piece, piece, piece, piece, piece, piece, piece,
            dma((nh, PIECES)), dma((nh, PIECES)),
            dma((ITERS, 4, 4)), dma((ITERS, 4, 4)),
            dma((nh, CHUNKS)), dma((nh, CHUNKS)),
            dma((nh, CHUNKS)), dma((nh, CHUNKS)),
            dma((nh, CHUNKS)), dma((nh, CHUNKS)),
            dma((nh, 2, 2)), dma((nh, 2, 2)),
            dma((nh, 2)), dma((nh, 2)),
            dma((nh,)), dma((nh,)),
            dma((nh,)), dma((nh,)),
        ],
        compiler_params=pltpu.CompilerParams(
            collective_id=0, has_side_effects=True, vmem_limit_bytes=62 * 1024 * 1024
        ),
    )(signal, demix.reshape(nb, high, 2, 2, rows, width2))
    direction = own - product
    return own + step_size * direction, direction


def solution(mesh):
    placed = (P("bin", None, None, "frame"), P("bin", None, None))
    return jax.shard_map(
        on_device,
        mesh=mesh,
        in_specs=placed,
        out_specs=(P("bin", "frame", None), P("bin", "frame", None)),
        check_vma=False,
    )
```

```python
import functools

import jax
import jax.numpy as jnp
from jax import lax
from jax.experimental import pallas as pl
from jax.experimental.pallas import tpu as pltpu
from jax.sharding import PartitionSpec as P

ITERS = 2
CHUNKS = 4
LAGS = (1,4,7)
PIECES = 4
EARLY = 6
AHEAD = 8

step_size = 0.05
small_eps = 1e-06

MESH = pl.DeviceIdType.MESH
NT = (((1,), (1,)), ((), ()))
f32 = jnp.float32
bf16 = jnp.bfloat16


def dot(a, b):
    return jnp.dot(a, b, preferred_element_type=f32)


def dot_nt(a, b):
    return lax.dot_general(a, b, NT, preferred_element_type=f32)


def kernel(
    group, bin_group, sig, w_in, w_out, p_out,
    xs, xr, xb, tmp, flat, w_next, w_hi, w_lo, src, yb, gram, r1, part, last, r2a, r2b, own, prod,
    power, rinv, pa_r, pb_s, pb_r, pc_s, pc_r, pd_s, pd_r,
    x_send, x_recv, pw_send, pw_recv, s1a_send, s1a_recv, s2a_send, s2a_recv, g_send, g_recv,
    s1b_send, s1b_recv, s2b_send, s2b_recv, wx_send, wx_recv, dx_send, dx_recv,
):
    nb, high, _, _, rows, width2 = w_in.shape
    width = width2 // 2
    nt = sig.shape[3]
    nh = nb // 2
    total = 4 * high * rows
    half = total // 2
    quarter = total // 4
    eighth = total // 8
    chunk = half // CHUNKS
    frames = nt * group
    bins = nb * bin_group
    me = lax.axis_index("frame")
    mb = lax.axis_index("bin")
    y = lax.rem(me, 2)
    lo = lax.rem(me // 2, 2)
    hi = me // 4
    near = high // 2
    hib = hi // near
    hir = lax.rem(hi, near)
    core = lax.rem(mb, 2)
    core_o = 1 - core
    y_dev = {"frame": me + 1 - 2 * y}
    lo_dev = {"frame": me + 2 - 4 * lo}
    core_dev = {"bin": mb + 1 - 2 * core}
    x_dev = {"bin": lax.rem(mb + 2, bin_group)}
    peers = [{"frame": lax.rem(hi + k, high) * 4 + lax.rem(me, 4)} for k in range(1, high)]

    def remote(a, b, s, r, dev):
        return pltpu.make_async_remote_copy(
            src_ref=a, dst_ref=b, send_sem=s, recv_sem=r, device_id=dev, device_id_type=MESH
        )

    def many(ref, sem):
        return pltpu.make_async_copy(ref, ref, sem)

    def x_copy(j, p):
        deep = 2 * sig.shape[2] // PIECES
        ref = lambda a: a.at[j, p // 2, pl.ds(pl.multiple_of(lax.rem(p, 2) * deep, deep), deep)]
        return remote(ref(xs), ref(xr), x_send.at[j, p], x_recv.at[j, p], lo_dev)

    def widen(j):
        xs[j] = sig[(1 - lo) * nh + j].astype(f32)

    barrier = pltpu.get_barrier_semaphore()
    for dev in [y_dev, lo_dev, core_dev, x_dev] + peers:
        pl.semaphore_signal(barrier, inc=1, device_id=dev, device_id_type=MESH)
    widen(0)
    pl.semaphore_wait(barrier, 4 + len(peers))
    for n in range(EARLY):
        if n % PIECES == 0 and n > 0:
            widen(n // PIECES)
        x_copy(n // PIECES, n % PIECES).start()

    def permute(f, to):
        for yd in range(2):
            for hd in range(high):
                for ld in range(2):
                    q = yd * 2 * high + hd // near * 2 * near + ld * near + hd % near
                    to[q * rows:(q + 1) * rows, :] = w_in[f, hd, ld, yd]

    def times(wr, wi, xr_, xi_):
        return dot(wr, xr_) - dot(wi, xi_), dot(wr, xi_) + dot(wi, xr_)

    def keep(j, b, yr, yi):
        src[j, b, 0] = yr
        src[j, b, 1] = yi
        yb[j, b, 0] = yr.astype(bf16)
        yb[j, b, 1] = yi.astype(bf16)

    def split(j, w):
        big = w.astype(bf16)
        w_hi[j] = big
        w_lo[j] = (w - big.astype(f32)).astype(bf16)

    power[...] = jnp.zeros_like(power)

    def first(j, carry):
        f = lo * nh + j
        permute(f, flat.at[j])
        split(j, flat[j])
        yr, yi = times(w_hi[j, :, :width], w_hi[j, :, width:], sig[f, 0], sig[f, 1])
        keep(j, lo, yr, yi)
        power[0, lo] += yr * yr + yi * yi
        f = (1 - lo) * nh + j
        permute(f, tmp)
        wr, wi = tmp[:, :width].astype(bf16), tmp[:, width:].astype(bf16)
        yr, yi = times(wr, wi, sig[f, 0], sig[f, 1])
        power[0, lo] += yr * yr + yi * yi
        return carry

    lax.fori_loop(0, nh, first, 0)

    def half_of(k):
        return y if k >= 2 else 1 - y

    def sub_of(k):
        return hib if k % 2 else 1 - hib

    def piece(k, who):
        return pl.ds(pl.multiple_of(half_of(k) * half + sub_of(k) * quarter + who * eighth, eighth), eighth)

    def pw(it, k, step, block):
        sems = pw_send.at[it, k, step], pw_recv.at[it, k, step]
        if step == 0:
            if it == 0:
                return remote(power.at[0, block, piece(k, core_o)], pa_r.at[0, k, block], *sems, core_dev)
            return remote(power.at[1, :, piece(k, core_o)], pa_r.at[1, k], *sems, core_dev)
        if step == 3:
            return remote(pd_s.at[it, k], pd_r.at[it, k], *sems, core_dev)
        a, b, dev = (pb_s, pb_r, x_dev) if step == 1 else (pc_s, pc_r, lo_dev)
        if it == 0:
            return remote(a.at[0, k, block], b.at[0, k, block], *sems, dev)
        return remote(a.at[1, k], b.at[1, k], *sems, dev)

    def pw_a(it, k):
        pw(it, k, 0, lo).start()

    def pw_b(it, k):
        pw(it, k, 0, lo).wait()
        if it == 0:
            pb_s[0, k, lo] = power[0, lo, piece(k, core), :] + pa_r[0, k, lo]
        else:
            for b in range(2):
                pb_s[1, k, b] = power[1, b, piece(k, core), :] + pa_r[1, k, b]
        pw(it, k, 1, lo).start()

    def pw_c(it, k):
        pw(it, k, 1, lo).wait()
        if it == 0:
            pc_s[0, k, lo] = pb_s[0, k, lo] + pb_r[0, k, lo]
        else:
            pc_s[1, k] = pb_s[1, k] + pb_r[1, k]
        pw(it, k, 2, lo).start()

    def inverse(p):
        return 1.0 / jnp.sqrt(p / bins + small_eps)

    def pw_d(it, k):
        pw(it, k, 2, lo).wait_send()
        pw(it, k, 2, 1 - lo).wait_recv()
        if it == 0:
            pd_s[0, k, lo] = pc_s[0, k, lo]
            pd_s[0, k, 1 - lo] = pc_r[0, k, 1 - lo]
        else:
            pd_s[1, k] = pc_s[1, k] + pc_r[1, k]
        pw(it, k, 3, lo).start()
        for b in range(2):
            rinv[b, piece(k, core), :] = inverse(pd_s[it, k, b])

    def pw_e(it, k):
        pw(it, k, 3, lo).wait()
        for b in range(2):
            rinv[b, piece(k, core_o), :] = inverse(pd_r[it, k, b])

    for k in range(4):
        pw_a(0, k)
    for k in range(4):
        pw_b(0, k)
    for k in range(4):
        pw_c(0, k)
    for j in range((EARLY + PIECES - 1) // PIECES, nh):
        widen(j)
    for n in range(EARLY, AHEAD):
        x_copy(n // PIECES, n % PIECES).start()
    for k in range(4):
        pw_d(0, k)
    for k in range(4):
        pw_e(0, k)

    def grams(j, its_rows):
        real = imag = None
        for b in range(2):
            inv = rinv[b, its_rows, :]
            pr = (src[j, b, 0, its_rows, :] * inv).astype(bf16)
            pi = (src[j, b, 1, its_rows, :] * inv).astype(bf16)
            br, bi = yb[j, b, 0], yb[j, b, 1]
            re = dot_nt(pr, br) + dot_nt(pi, bi)
            im = dot_nt(pi, br) - dot_nt(pr, bi)
            real, imag = (re, im) if b == 0 else (real + re, imag + im)
        return real, imag

    def triple(acc, j):
        n = acc.shape[0]
        both = jnp.concatenate([acc[:, :width], acc[:, width:]], axis=0)
        big = both.astype(bf16)
        small = (both - big.astype(f32)).astype(bf16)
        out = dot(big, w_hi[j]) + (dot(small, w_hi[j]) + dot(big, w_lo[j]))
        a, b = out[:n], out[n:]
        return a[:, :width] - b[:, width:], a[:, width:] + b[:, :width]

    def at(c):
        return pl.ds(pl.multiple_of(c * chunk, chunk), chunk)

    def at_own(c):
        return pl.ds(pl.multiple_of(y * half + c * chunk, chunk), chunk)

    def at_other(c):
        return pl.ds(pl.multiple_of((1 - y) * half + c * chunk, chunk), chunk)

    def s1a(j, c):
        return remote(gram.at[0, j, 1 - y, at(c)], r1.at[0, j, at(c)], s1a_send.at[j, c], s1a_recv.at[j, c], y_dev)

    def s2a(j, c, k):
        return remote(part.at[j, at(c)], r2a.at[j, c, k - 1], s2a_send.at[j, c], s2a_recv.at[j, c], peers[k - 1])

    def g(j, its_rows, c):
        ref = w_next.at[j, its_rows]
        return remote(ref, ref, g_send.at[j, c], g_recv.at[j, c], y_dev)

    def arrive(j):
        for p in range(PIECES):
            x_copy(j, p).wait_recv()
        xb[j] = xr[j].astype(bf16)
        yr, yi = times(w_hi[j, :, :width], w_hi[j, :, width:], xb[j, 0], xb[j, 1])
        keep(j, 1 - lo, yr, yi)
        for away in range(2):
            h = y if away else 1 - y
            real, imag = grams(j, pl.ds(pl.multiple_of(h * half, half), half))
            gram[0, j, h, :, :width] = real
            gram[0, j, h, :, width:] = imag
            if away == 0:
                for c in range(CHUNKS):
                    s1a(j, c).start()

    def sum1(j, c):
        s1a(j, c).wait_recv()
        part[j, at(c)] = gram[0, j, y, at(c)] + r1[0, j, at(c)]
        for k in range(1, high):
            s2a(j, c, k).start()
        n = j * CHUNKS + c + AHEAD
        pl.when(n < nh * PIECES)(lambda: x_copy(n // PIECES, lax.rem(n, PIECES)).start())

    def update(j, c):
        many(r2a.at[j, c], s2a_recv.at[j, c]).wait()
        acc = part[j, at(c)]
        for k in range(high - 1):
            acc = acc + r2a[j, c, k]
        ar, ai = triple(acc * (1.0 / frames), j)
        w = flat[j, at_own(c)]
        wr, wi = w[:, :width], w[:, width:]
        w_next[j, at_own(c), :width] = wr + step_size * (wr - ar)
        w_next[j, at_own(c), width:] = wi + step_size * (wi - ai)
        g(j, at_own(c), c).start()

    def wx(j, from_lo):
        return remote(own.at[j, 1 - lo], w_out.at[from_lo * nh + j], wx_send.at[j], wx_recv.at[j], lo_dev)

    def mine(j):
        start = pl.multiple_of(y * half + hib * quarter, quarter)
        w = w_next[j, pl.ds(start, quarter), :]
        for l in range(2):
            for r in range(near):
                q = l * near + r
                if near == 1:
                    own[j, l] = w[q * rows:(q + 1) * rows]
                else:
                    pl.when(hir == r)(functools.partial(place, j, l, w[q * rows:(q + 1) * rows]))
        wx(j, lo).start()
        w_out[lo * nh + j] = own[j, lo]

    def place(j, l, w):
        own[j, l] = w

    def second(j):
        for c in range(CHUNKS):
            g(j, at_other(c), c).wait_recv()
        split(j, w_next[j])
        wr, wi = w_hi[j, :, :width], w_hi[j, :, width:]
        for b in range(2):
            yr, yi = times(wr, wi, *((sig[lo * nh + j, 0], sig[lo * nh + j, 1]) if b == 0 else (xb[j, 0], xb[j, 1])))
            block = lo if b == 0 else 1 - lo
            keep(j, block, yr, yi)
            power[1, block] += yr * yr + yi * yi
        mine(j)

    units = nh * CHUNKS

    def pipeline(s, carry):
        def on(lag, stage):
            u = s - lag
            j, c = u // CHUNKS, lax.rem(u, CHUNKS)
            pl.when(jnp.logical_and(u >= 0, u < units))(lambda: stage(j, c))

        on(LAGS[0], sum1)
        on(LAGS[1], update)
        on(0, lambda j, c: pl.when(c == 0)(lambda: arrive(j)))
        on(LAGS[2], lambda j, c: pl.when(c == CHUNKS - 1)(lambda: second(j)))
        return carry

    lax.fori_loop(0, units + LAGS[2], pipeline, 0)

    for k in range(4):
        pw_a(1, k)

    def dx(j, from_lo):
        return remote(prod.at[j], p_out.at[from_lo * nh + j], dx_send.at[j], dx_recv.at[j], lo_dev)

    def at_piece(i, l):
        sub = hib if i else 1 - hib
        side = lo if l else 1 - lo
        return pl.ds(pl.multiple_of(sub * quarter + side * eighth, eighth), eighth)

    def s1b(j, i, l):
        its = at_piece(i, l)
        return remote(gram.at[1, j, 1 - y, its], r1.at[1, j, its], s1b_send.at[j, i, l], s1b_recv.at[j, i, l], y_dev)

    def s2b(j, l, k):
        target = lax.rem(hi + k, high)
        return remote(
            last.at[j, l, target], r2b.at[j, l, k - 1], s2b_send.at[j, l], s2b_recv.at[j, l], peers[k - 1]
        )

    def make_gram(k, j):
        h, sub = half_of(k), sub_of(k)
        real, imag = grams(j, pl.ds(pl.multiple_of(h * half + sub * quarter, quarter), quarter))
        its = pl.ds(pl.multiple_of(sub * quarter, quarter), quarter)
        gram[1, j, h, its, :width] = real
        gram[1, j, h, its, width:] = imag

    def sum1b(j, i, l):
        s1b(j, i, l).wait_recv()
        its = at_piece(i, l)
        value = gram[1, j, y, its] + r1[1, j, its]
        sub = hib if i else 1 - hib
        for r in range(near):
            last[j, l, sub * near + r] = value[r * rows:(r + 1) * rows]
        for k in range(1, high):
            there = lax.rem(hi + k, high) // near == sub
            pl.when(there)(lambda k=k: s2b(j, l, k).start())

    def each(stage):
        def body(j, carry):
            stage(j)
            return carry

        lax.fori_loop(0, nh, body, 0)

    for k in range(4):
        pw_b(1, k)
    pw_c(1, 0)
    pw_c(1, 1)
    pw_c(1, 2)
    pw_d(1, 0)
    pw_c(1, 3)
    pw_e(1, 0)

    def gram_away(i, j):
        make_gram(i, j)
        s1b(j, i, 0).start()

    each(functools.partial(gram_away, 0))
    pw_d(1, 1)
    pw_e(1, 1)
    each(functools.partial(gram_away, 1))
    for i in range(2):
        each(lambda j, i=i: s1b(j, i, 1).start())
    pw_d(1, 2)
    pw_e(1, 2)

    def gram_own(j):
        make_gram(2, j)
        sum1b(j, 0, 0)

    each(gram_own)
    pw_d(1, 3)
    pw_e(1, 3)
    each(functools.partial(make_gram, 3))

    def finish(j, l):
        many(r2b.at[j, l], s2b_recv.at[j, l]).wait()
        acc = last[j, l, hi]
        for k in range(high - 1):
            acc = acc + r2b[j, l, k]
        ar, ai = triple(acc * (1.0 / frames), j)
        if l == 0:
            prod[j, :, :width] = ar
            prod[j, :, width:] = ai
            dx(j, lo).start()
        else:
            p_out[lo * nh + j, :, :width] = ar
            p_out[lo * nh + j, :, width:] = ai

    def close0(j):
        sum1b(j, 1, 0)
        finish(j, 0)
        sum1b(j, 0, 1)

    def close1(j):
        sum1b(j, 1, 1)
        finish(j, 1)

    each(close0)
    each(close1)

    def drain(j):
        for p in range(PIECES):
            x_copy(j, p).wait_send()
        for c in range(CHUNKS):
            s1a(j, c).wait_send()
            many(r2a.at[j, c], s2a_send.at[j, c]).wait()
            g(j, at_own(c), c).wait_send()
        for l in range(2):
            for i in range(2):
                s1b(j, i, l).wait_send()
            many(r2b.at[j, l], s2b_send.at[j, l]).wait()
        wx(j, lo).wait_send()
        wx(j, 1 - lo).wait_recv()
        dx(j, lo).wait_send()
        dx(j, 1 - lo).wait_recv()

    each(drain)


def on_device(signal, demix):
    group = lax.axis_size("frame")
    bin_group = lax.axis_size("bin")
    nb, _, sensors, nt = signal.shape
    total, width2 = demix.shape[1:]
    rows = total // group
    high = group // 4
    half = total // 2
    eighth = total // 8
    nh = nb // 2
    out = jax.ShapeDtypeStruct((nb, rows, width2), f32)
    dma = pltpu.SemaphoreType.DMA
    vmem = pl.BlockSpec(memory_space=pltpu.VMEM)
    piece = pltpu.VMEM((ITERS, 4, 2, eighth, nt), f32)
    own, product = pl.pallas_call(
        functools.partial(kernel, group, bin_group),
        out_shape=(out, out),
        in_specs=[vmem, vmem],
        out_specs=(vmem, vmem),
        scratch_shapes=[
            pltpu.VMEM((nh, 2, sensors, nt), f32),
            pltpu.VMEM((nh, 2, sensors, nt), f32),
            pltpu.VMEM((nh, 2, sensors, nt), bf16),
            pltpu.VMEM((total, width2), f32),
            pltpu.VMEM((nh, total, width2), f32),
            pltpu.VMEM((nh, total, width2), f32),
            pltpu.VMEM((nh, total, width2), bf16),
            pltpu.VMEM((nh, total, width2), bf16),
            pltpu.VMEM((nh, 2, 2, total, nt), f32),
            pltpu.VMEM((nh, 2, 2, total, nt), bf16),
            pltpu.VMEM((ITERS, nh, 2, half, width2), f32),
            pltpu.VMEM((ITERS, nh, half, width2), f32),
            pltpu.VMEM((nh, half, width2), f32),
            pltpu.VMEM((nh, 2, high, rows, width2), f32),
            pltpu.VMEM((nh, CHUNKS, high - 1, half // CHUNKS, width2), f32),
            pltpu.VMEM((nh, 2, high - 1, rows, width2), f32),
            pltpu.VMEM((nh, 2, rows, width2), f32),
            pltpu.VMEM((nh, rows, width2), f32),
            pltpu.VMEM((ITERS, 2, total, nt), f32),
            pltpu.VMEM((2, total, nt), f32),
            piece, piece, piece, piece, piece, piece, piece,
            dma((nh, PIECES)), dma((nh, PIECES)),
            dma((ITERS, 4, 4)), dma((ITERS, 4, 4)),
            dma((nh, CHUNKS)), dma((nh, CHUNKS)),
            dma((nh, CHUNKS)), dma((nh, CHUNKS)),
            dma((nh, CHUNKS)), dma((nh, CHUNKS)),
            dma((nh, 2, 2)), dma((nh, 2, 2)),
            dma((nh, 2)), dma((nh, 2)),
            dma((nh,)), dma((nh,)),
            dma((nh,)), dma((nh,)),
        ],
        compiler_params=pltpu.CompilerParams(
            collective_id=0, has_side_effects=True, vmem_limit_bytes=62 * 1024 * 1024
        ),
    )(signal, demix.reshape(nb, high, 2, 2, rows, width2))
    direction = own - product
    return own + step_size * direction, direction


def solution(mesh):
    placed = (P("bin", None, None, "frame"), P("bin", None, None))
    return jax.shard_map(
        on_device,
        mesh=mesh,
        in_specs=placed,
        out_specs=(P("bin", "frame", None), P("bin", "frame", None)),
        check_vma=False,
    )
```

```python
import functools

import jax
import jax.numpy as jnp
from jax import lax
from jax.experimental import pallas as pl
from jax.experimental.pallas import tpu as pltpu
from jax.sharding import PartitionSpec as P

ITERS = 2
CHUNKS = 4
ORDER = (0, 2, 1, 3)
BEHIND = 2
LAGS = (1, 4, 6)
PIECES = 4
EARLY = 4
AHEAD = 9

step_size = 0.05
small_eps = 1e-06

MESH = pl.DeviceIdType.MESH
NT = (((1,), (1,)), ((), ()))
f32 = jnp.float32
bf16 = jnp.bfloat16


def dot(a, b):
    return jnp.dot(a, b, preferred_element_type=f32)


def dot_nt(a, b):
    return lax.dot_general(a, b, NT, preferred_element_type=f32)


def kernel(
    group, bin_group, sig_hbm, w_hbm, w_out, p_out,
    sig, w_in, xs, xr, xb, tmp, flat, w_next, w_hi, w_lo, v_hi, v_lo, src, yb,
    gram, r1, part, r2a, gram_b, r1b, last, r2b, own, prod,
    power, rinv, pa_r, pb_s, pb_r, pc_s, pc_r, pd_s, pd_r,
    x_send, x_recv, pw_send, pw_recv, s1a_send, s1a_recv, s2a_send, s2a_recv, g_send, g_recv,
    s1b_send, s1b_recv, s2b_send, s2b_recv, wx_send, wx_recv, dx_send, dx_recv, sig_sem, w_sem,
):
    nb, high, _, _, rows, width2 = w_in.shape
    width = width2 // 2
    nt = sig.shape[3]
    nh = nb // 2
    total = 4 * high * rows
    half = total // 2
    quarter = total // 4
    eighth = total // 8
    chunk = half // CHUNKS
    frames = nt * group
    bins = nb * bin_group
    me = lax.axis_index("frame")
    mb = lax.axis_index("bin")
    y = lax.rem(me, 2)
    lo = lax.rem(me // 2, 2)
    hi = me // 4
    near = high // 2
    hib = hi // near
    hir = lax.rem(hi, near)
    core = lax.rem(mb, 2)
    core_o = 1 - core
    y_dev = {"frame": me + 1 - 2 * y}
    lo_dev = {"frame": me + 2 - 4 * lo}
    core_dev = {"bin": mb + 1 - 2 * core}
    x_dev = {"bin": lax.rem(mb + 2, bin_group)}
    peers = [{"frame": lax.rem(hi + k, high) * 4 + lax.rem(me, 4)} for k in range(1, high)]

    def remote(a, b, s, r, dev):
        return pltpu.make_async_remote_copy(
            src_ref=a, dst_ref=b, send_sem=s, recv_sem=r, device_id=dev, device_id_type=MESH
        )

    def many(ref, sem):
        return pltpu.make_async_copy(ref, ref, sem)

    def x_copy(j, p):
        deep = 2 * sig.shape[2] // PIECES
        ref = lambda a: a.at[j, p // 2, pl.ds(pl.multiple_of(lax.rem(p, 2) * deep, deep), deep)]
        return remote(ref(xs), ref(xr), x_send.at[j, p], x_recv.at[j, p], lo_dev)

    def load_sig(f):
        return pltpu.make_async_copy(sig_hbm.at[f], sig.at[f], sig_sem.at[f])

    def load_w(f):
        return pltpu.make_async_copy(w_hbm.at[f], w_in.at[f], w_sem.at[f])

    def widen(j):
        f = (1 - lo) * nh + j
        load_sig(f).wait()
        xs[j] = sig[f].astype(f32)

    for j in range(nh):
        load_sig((1 - lo) * nh + j).start()
    barrier = pltpu.get_barrier_semaphore()
    for dev in [y_dev, lo_dev, core_dev, x_dev] + peers:
        pl.semaphore_signal(barrier, inc=1, device_id=dev, device_id_type=MESH)
    for j in range(nh):
        load_sig(lo * nh + j).start()
        load_w(lo * nh + j).start()
        load_w((1 - lo) * nh + j).start()
    power[...] = jnp.zeros_like(power)
    for j in range(nh):
        widen(j)
    pl.semaphore_wait(barrier, 4 + len(peers))
    for n in range(EARLY):
        x_copy(n // PIECES, n % PIECES).start()

    def permute(f, to):
        for yd in range(2):
            for hd in range(high):
                for ld in range(2):
                    q = yd * 2 * high + hd // near * 2 * near + ld * near + hd % near
                    to[q * rows:(q + 1) * rows, :] = w_in[f, hd, ld, yd]

    def times(wr, wi, xr_, xi_):
        return dot(wr, xr_) - dot(wi, xi_), dot(wr, xi_) + dot(wi, xr_)

    def keep(j, b, yr, yi):
        src[j, b, 0] = yr
        src[j, b, 1] = yi
        yb[j, b, 0] = yr.astype(bf16)
        yb[j, b, 1] = yi.astype(bf16)

    def split(j, w):
        big = w.astype(bf16)
        w_hi[j] = big
        w_lo[j] = (w - big.astype(f32)).astype(bf16)

    def first(j, carry):
        f = lo * nh + j
        load_sig(f).wait()
        load_w(f).wait()
        load_w((1 - lo) * nh + j).wait()
        permute(f, flat.at[j])
        split(j, flat[j])
        yr, yi = times(w_hi[j, :, :width], w_hi[j, :, width:], sig[f, 0], sig[f, 1])
        keep(j, lo, yr, yi)
        power[0, lo] += yr * yr + yi * yi
        f = (1 - lo) * nh + j
        permute(f, tmp)
        wr, wi = tmp[:, :width].astype(bf16), tmp[:, width:].astype(bf16)
        yr, yi = times(wr, wi, sig[f, 0], sig[f, 1])
        power[0, lo] += yr * yr + yi * yi
        return carry

    lax.fori_loop(0, nh, first, 0)

    def piece(k, who):
        return pl.ds(pl.multiple_of(who * half + ORDER[k] * chunk, chunk), chunk)

    def pw(it, k, step, block):
        sems = pw_send.at[it, k, step], pw_recv.at[it, k, step]
        if step == 0:
            if it == 0:
                return remote(power.at[0, block, piece(k, core_o)], pa_r.at[0, k, block], *sems, core_dev)
            return remote(power.at[1, :, piece(k, core_o)], pa_r.at[1, k], *sems, core_dev)
        if step == 3:
            return remote(pd_s.at[it, k], pd_r.at[it, k], *sems, core_dev)
        a, b, dev = (pb_s, pb_r, x_dev) if step == 1 else (pc_s, pc_r, lo_dev)
        if it == 0:
            return remote(a.at[0, k, block], b.at[0, k, block], *sems, dev)
        return remote(a.at[1, k], b.at[1, k], *sems, dev)

    def pw_a(it, k):
        pw(it, k, 0, lo).start()

    def pw_b(it, k):
        pw(it, k, 0, lo).wait()
        if it == 0:
            pb_s[0, k, lo] = power[0, lo, piece(k, core), :] + pa_r[0, k, lo]
        else:
            for b in range(2):
                pb_s[1, k, b] = power[1, b, piece(k, core), :] + pa_r[1, k, b]
        pw(it, k, 1, lo).start()

    def pw_c(it, k):
        pw(it, k, 1, lo).wait()
        if it == 0:
            pc_s[0, k, lo] = pb_s[0, k, lo] + pb_r[0, k, lo]
        else:
            pc_s[1, k] = pb_s[1, k] + pb_r[1, k]
        pw(it, k, 2, lo).start()

    def inverse(p):
        return 1.0 / jnp.sqrt(p / bins + small_eps)

    def pw_d(it, k):
        pw(it, k, 2, lo).wait_send()
        pw(it, k, 2, 1 - lo).wait_recv()
        if it == 0:
            pd_s[0, k, lo] = pc_s[0, k, lo]
            pd_s[0, k, 1 - lo] = pc_r[0, k, 1 - lo]
        else:
            pd_s[1, k] = pc_s[1, k] + pc_r[1, k]
        pw(it, k, 3, lo).start()
        for b in range(2):
            rinv[b, piece(k, core), :] = inverse(pd_s[it, k, b])

    def pw_e(it, k):
        pw(it, k, 3, lo).wait()
        for b in range(2):
            rinv[b, piece(k, core_o), :] = inverse(pd_r[it, k, b])

    for k in range(4):
        pw_a(0, k)
    for k in range(4):
        pw_b(0, k)
    for k in range(4):
        pw_c(0, k)
    for n in range(EARLY, AHEAD):
        x_copy(n // PIECES, n % PIECES).start()
    for k in range(4):
        pw_d(0, k)
    for k in range(4):
        pw_e(0, k)

    def grams(j, slices):
        real = imag = None
        for b in range(2):
            scored = []
            for i in range(2):
                parts = [(src[j, b, i, its, :] * rinv[b, its, :]).astype(bf16) for its in slices]
                scored.append(jnp.concatenate(parts, axis=0) if len(parts) > 1 else parts[0])
            pr, pi = scored
            br, bi = yb[j, b, 0], yb[j, b, 1]
            re = dot_nt(pr, br) + dot_nt(pi, bi)
            im = dot_nt(pi, br) - dot_nt(pr, bi)
            real, imag = (re, im) if b == 0 else (real + re, imag + im)
        return real, imag

    def triple(acc, m_hi, m_lo):
        n = acc.shape[0]
        both = jnp.concatenate([acc[:, :width], acc[:, width:]], axis=0)
        big = both.astype(bf16)
        small = (both - big.astype(f32)).astype(bf16)
        out = dot(big, m_hi[...]) + (dot(small, m_hi[...]) + dot(big, m_lo[...]))
        a, b = out[:n], out[n:]
        return a[:, :width] - b[:, width:], a[:, width:] + b[:, :width]

    def at(c):
        return pl.ds(pl.multiple_of(c * chunk, chunk), chunk)

    def at_own(c):
        return pl.ds(pl.multiple_of(y * half + c * chunk, chunk), chunk)

    def at_other(c):
        return pl.ds(pl.multiple_of((1 - y) * half + c * chunk, chunk), chunk)

    def s1a(j, c):
        return remote(gram.at[j, 1 - y, at(c)], r1.at[j, at(c)], s1a_send.at[j, c], s1a_recv.at[j, c], y_dev)

    def s2a(j, c, k):
        return remote(part.at[j, at(c)], r2a.at[j, c, k - 1], s2a_send.at[j, c], s2a_recv.at[j, c], peers[k - 1])

    def g(j, its_rows, c):
        ref = w_next.at[j, its_rows]
        return remote(ref, ref, g_send.at[j, c], g_recv.at[j, c], y_dev)

    def arrive(j):
        for p in range(PIECES):
            x_copy(j, p).wait_recv()
        xb[j] = xr[j].astype(bf16)
        yr, yi = times(w_hi[j, :, :width], w_hi[j, :, width:], xb[j, 0], xb[j, 1])
        keep(j, 1 - lo, yr, yi)
        for away in range(2):
            h = y if away else 1 - y
            real, imag = grams(j, [pl.ds(pl.multiple_of(h * half, half), half)])
            gram[j, h, :, :width] = real
            gram[j, h, :, width:] = imag
            if away == 0:
                for c in ORDER:
                    s1a(j, c).start()

    def sum1(j, t, c):
        s1a(j, c).wait_recv()
        part[j, at(c)] = gram[j, y, at(c)] + r1[j, at(c)]
        for k in range(1, high):
            s2a(j, c, k).start()
        n = j * CHUNKS + t + AHEAD
        pl.when(n < nh * PIECES)(lambda: x_copy(n // PIECES, lax.rem(n, PIECES)).start())

    def update(j, t, c):
        many(r2a.at[j, c], s2a_recv.at[j, c]).wait()
        acc = part[j, at(c)]
        for k in range(high - 1):
            acc = acc + r2a[j, c, k]
        ar, ai = triple(acc * (1.0 / frames), w_hi.at[j], w_lo.at[j])
        w = flat[j, at_own(c)]
        wr, wi = w[:, :width], w[:, width:]
        w_next[j, at_own(c), :width] = wr + step_size * (wr - ar)
        w_next[j, at_own(c), width:] = wi + step_size * (wi - ai)
        g(j, at_own(c), c).start()

    def wx(j, from_lo):
        return remote(own.at[j, 1 - lo], w_out.at[from_lo * nh + j], wx_send.at[j], wx_recv.at[j], lo_dev)

    def mine(j):
        start = pl.multiple_of(y * half + hib * quarter, quarter)
        w = w_next[j, pl.ds(start, quarter), :]
        for l in range(2):
            for r in range(near):
                q = l * near + r
                if near == 1:
                    own[j, l] = w[q * rows:(q + 1) * rows]
                else:
                    pl.when(hir == r)(functools.partial(place, j, l, w[q * rows:(q + 1) * rows]))
        wx(j, lo).start()
        w_out[lo * nh + j] = own[j, lo]

    def place(j, l, w):
        own[j, l] = w

    def second(j, t, c):
        g(j, at_other(c), c).wait_recv()
        both = [at(c), pl.ds(pl.multiple_of(half + c * chunk, chunk), chunk)]
        w = jnp.concatenate([w_next[j, its] for its in both], axis=0)
        big = w.astype(bf16)
        small = (w - big.astype(f32)).astype(bf16)
        for h, its in enumerate(both):
            v_hi[j, its] = big[h * chunk:(h + 1) * chunk]
            v_lo[j, its] = small[h * chunk:(h + 1) * chunk]
        for b in range(2):
            x = (sig[lo * nh + j, 0], sig[lo * nh + j, 1]) if b == 0 else (xb[j, 0], xb[j, 1])
            yr, yi = times(big[:, :width], big[:, width:], *x)
            block = lo if b == 0 else 1 - lo
            squares = yr * yr + yi * yi
            for h, its in enumerate(both):
                here = slice(h * chunk, (h + 1) * chunk)
                src[j, block, 0, its] = yr[here]
                src[j, block, 1, its] = yi[here]
                yb[j, block, 0, its] = yr[here].astype(bf16)
                yb[j, block, 1, its] = yi[here].astype(bf16)
                power[1, block, its] += squares[here]

    units = nh * CHUNKS

    def stage_of(u):
        j, t = u // CHUNKS, lax.rem(u, CHUNKS)
        return j, t, lax.rem(t, 2) * 2 + t // 2

    def pipeline(s, carry):
        def on(lag, stage):
            u = s - lag
            pl.when(jnp.logical_and(u >= 0, u < units))(lambda: stage(*stage_of(u)))

        on(LAGS[0], sum1)
        on(LAGS[1], update)
        on(0, lambda j, t, c: pl.when(t == 0)(lambda: arrive(j)))
        on(LAGS[2], second)
        on(LAGS[2], lambda j, t, c: pl.when(t == CHUNKS - 1)(lambda: mine(j)))
        return carry

    lax.fori_loop(0, units, pipeline, 0)

    def run(stage, u):
        j, t = u // CHUNKS, u % CHUNKS
        stage(j, t, ORDER[t])

    for u in range(units - LAGS[0], units):
        run(sum1, u)
    tail = units - CHUNKS
    for u in range(units - LAGS[1], tail):
        run(update, u)
    for u in range(units - LAGS[2], tail):
        run(second, u)
        if u % CHUNKS == CHUNKS - 1:
            mine(u // CHUNKS)
    run(update, tail)
    run(update, tail + 1)
    run(second, tail)
    pw_a(1, 0)
    pw_b(1, 0)
    run(update, tail + 2)
    run(second, tail + 1)
    pw_a(1, 1)
    pw_b(1, 1)
    pw_c(1, 0)
    run(update, tail + 3)
    run(second, tail + 2)
    pw_a(1, 2)
    pw_b(1, 2)
    mine(nh - 1)
    pw_c(1, 1)
    pw_d(1, 0)
    pw_e(1, 0)
    run(second, tail + 3)
    pw_a(1, 3)
    pw_b(1, 3)
    pw_c(1, 2)
    pw_d(1, 1)
    pw_e(1, 1)

    def dx(j, from_lo):
        return remote(prod.at[j], p_out.at[from_lo * nh + j], dx_send.at[j], dx_recv.at[j], lo_dev)

    def step_of(p):
        m = p // (nh // 2)
        inner = lax.rem((m + 1) // 2, 2)
        j = lo * lax.rem(p, nh) + (1 - lo) * (p - nh // 2 * inner - nh * (m // 3))
        return j, lo * (p // nh) + (1 - lo) * inner

    def s1b(j, l, i):
        return remote(
            gram_b.at[j, l, 0, i], r1b.at[j, l, i], s1b_send.at[j, l, i], s1b_recv.at[j, l, i], y_dev
        )

    def s2b(j, l, k):
        target = lax.rem(hi + k, high)
        i = 1 - lax.rem(target // near + hib, 2)
        return remote(
            last.at[j, l, i, lax.rem(target, near)], r2b.at[j, l, k - 1],
            s2b_send.at[j, l], s2b_recv.at[j, l], peers[k - 1],
        )

    def make_gram(p):
        j, l = step_of(p)
        slices = []
        for h in (1 - y, y):
            for sub in (1 - hib, hib):
                slices.append(pl.ds(pl.multiple_of(h * half + sub * quarter + l * eighth, eighth), eighth))
        real, imag = grams(j, slices)
        for h in range(2):
            for i in range(2):
                q = h * 2 + i
                gram_b[j, l, h, i, :, :width] = real[q * eighth:(q + 1) * eighth]
                gram_b[j, l, h, i, :, width:] = imag[q * eighth:(q + 1) * eighth]
        s1b(j, l, 0).start()
        s1b(j, l, 1).start()

    def sum1b(j, l, i):
        s1b(j, l, i).wait_recv()
        value = gram_b[j, l, 1, i] + r1b[j, l, i]
        for r in range(near):
            last[j, l, i, r] = value[r * rows:(r + 1) * rows]
        for k in range(1, high):
            there = lax.rem(lax.rem(hi + k, high) // near + hib, 2) == 1 - i
            pl.when(there)(lambda k=k: s2b(j, l, k).start())

    def send_on(p):
        j, l = step_of(p)
        sum1b(j, l, 0)

    def finish(p):
        j, l = step_of(p)
        sum1b(j, l, 1)
        many(r2b.at[j, l], s2b_recv.at[j, l]).wait()
        acc = last[j, l, 1, hir]
        for k in range(high - 1):
            acc = acc + r2b[j, l, k]
        ar, ai = triple(acc * (1.0 / frames), v_hi.at[j], v_lo.at[j])

        @pl.when(l != lo)
        def _():
            prod[j, :, :width] = ar
            prod[j, :, width:] = ai
            dx(j, lo).start()

        @pl.when(l == lo)
        def _():
            p_out[lo * nh + j, :, :width] = ar
            p_out[lo * nh + j, :, width:] = ai

    def each(stage, start, stop):
        def body(p, carry):
            stage(p)
            return carry

        lax.fori_loop(start, stop, body, 0)

    steps = 2 * nh
    each(make_gram, 0, 2)
    pw_c(1, 3)
    pw_d(1, 2)
    pw_e(1, 2)
    each(send_on, 0, 1)
    pw_d(1, 3)
    pw_e(1, 3)
    each(make_gram, 2, steps)

    def both(p):
        pl.when(p < steps)(lambda: send_on(p))
        finish(p - BEHIND)

    each(send_on, 1, BEHIND)
    each(both, BEHIND, steps + BEHIND)

    def drain(j):
        for p in range(PIECES):
            x_copy(j, p).wait_send()
        for c in range(CHUNKS):
            s1a(j, c).wait_send()
            many(r2a.at[j, c], s2a_send.at[j, c]).wait()
            g(j, at_own(c), c).wait_send()
        for l in range(2):
            for i in range(2):
                s1b(j, l, i).wait_send()
            many(r2b.at[j, l], s2b_send.at[j, l]).wait()
        wx(j, lo).wait_send()
        wx(j, 1 - lo).wait_recv()
        dx(j, lo).wait_send()
        dx(j, 1 - lo).wait_recv()

    each(drain, 0, nh)


def on_device(signal, demix):
    group = lax.axis_size("frame")
    bin_group = lax.axis_size("bin")
    nb, _, sensors, nt = signal.shape
    total, width2 = demix.shape[1:]
    rows = total // group
    high = group // 4
    half = total // 2
    eighth = total // 8
    nh = nb // 2
    out = jax.ShapeDtypeStruct((nb, rows, width2), f32)
    dma = pltpu.SemaphoreType.DMA
    vmem = pl.BlockSpec(memory_space=pltpu.VMEM)
    hbm = pl.BlockSpec(memory_space=pl.ANY)
    piece = pltpu.VMEM((ITERS, 4, 2, eighth, nt), f32)
    own, product = pl.pallas_call(
        functools.partial(kernel, group, bin_group),
        out_shape=(out, out),
        in_specs=[hbm, hbm],
        out_specs=(vmem, vmem),
        scratch_shapes=[
            pltpu.VMEM((nb, 2, sensors, nt), bf16),
            pltpu.VMEM((nb, high, 2, 2, rows, width2), f32),
            pltpu.VMEM((nh, 2, sensors, nt), f32),
            pltpu.VMEM((nh, 2, sensors, nt), f32),
            pltpu.VMEM((nh, 2, sensors, nt), bf16),
            pltpu.VMEM((total, width2), f32),
            pltpu.VMEM((nh, total, width2), f32),
            pltpu.VMEM((nh, total, width2), f32),
            pltpu.VMEM((nh, total, width2), bf16),
            pltpu.VMEM((nh, total, width2), bf16),
            pltpu.VMEM((nh, total, width2), bf16),
            pltpu.VMEM((nh, total, width2), bf16),
            pltpu.VMEM((nh, 2, 2, total, nt), f32),
            pltpu.VMEM((nh, 2, 2, total, nt), bf16),
            pltpu.VMEM((nh, 2, half, width2), f32),
            pltpu.VMEM((nh, half, width2), f32),
            pltpu.VMEM((nh, half, width2), f32),
            pltpu.VMEM((nh, CHUNKS, high - 1, half // CHUNKS, width2), f32),
            pltpu.VMEM((nh, 2, 2, 2, eighth, width2), f32),
            pltpu.VMEM((nh, 2, 2, eighth, width2), f32),
            pltpu.VMEM((nh, 2, 2, high // 2, rows, width2), f32),
            pltpu.VMEM((nh, 2, high - 1, rows, width2), f32),
            pltpu.VMEM((nh, 2, rows, width2), f32),
            pltpu.VMEM((nh, rows, width2), f32),
            pltpu.VMEM((ITERS, 2, total, nt), f32),
            pltpu.VMEM((2, total, nt), f32),
            piece, piece, piece, piece, piece, piece, piece,
            dma((nh, PIECES)), dma((nh, PIECES)),
            dma((ITERS, 4, 4)), dma((ITERS, 4, 4)),
            dma((nh, CHUNKS)), dma((nh, CHUNKS)),
            dma((nh, CHUNKS)), dma((nh, CHUNKS)),
            dma((nh, CHUNKS)), dma((nh, CHUNKS)),
            dma((nh, 2, 2)), dma((nh, 2, 2)),
            dma((nh, 2)), dma((nh, 2)),
            dma((nh,)), dma((nh,)),
            dma((nh,)), dma((nh,)),
            dma((nb,)), dma((nb,)),
        ],
        compiler_params=pltpu.CompilerParams(
            collective_id=0, has_side_effects=True, vmem_limit_bytes=62 * 1024 * 1024
        ),
    )(signal, demix.reshape(nb, high, 2, 2, rows, width2))
    direction = own - product
    return own + step_size * direction, direction


def solution(mesh):
    placed = (P("bin", None, None, "frame"), P("bin", None, None))
    return jax.shard_map(
        on_device,
        mesh=mesh,
        in_specs=placed,
        out_specs=(P("bin", "frame", None), P("bin", "frame", None)),
        check_vma=False,
    )
```

```python
import functools

import jax
import jax.numpy as jnp
from jax import lax
from jax.experimental import pallas as pl
from jax.experimental.pallas import tpu as pltpu
from jax.sharding import PartitionSpec as P

ITERS = 2
CHUNKS = 4
ORDER = (0, 2, 1, 3)
BEHIND = 2
LAGS = (1, 4, 6)
PIECES = 4
EARLY = 4
AHEAD = 9

step_size = 0.05
small_eps = 1e-06

MESH = pl.DeviceIdType.MESH
NT = (((1,), (1,)), ((), ()))
f32 = jnp.float32
bf16 = jnp.bfloat16


def dot(a, b):
    return jnp.dot(a, b, preferred_element_type=f32)


def dot_nt(a, b):
    return lax.dot_general(a, b, NT, preferred_element_type=f32)


def kernel(
    group, bin_group, sig_hbm, w_hbm, w_out, p_out,
    sig, w_in, xs, xr, xb, tmp, flat, w_next, w_hi, w_lo, v_hi, v_lo, src, yb,
    gram, r1, part, r2a, gram_b, r1b, last, r2b, own, prod, kept,
    power, rinv, pa_r, pb_s, pb_r, pc_s, pc_r, pd_s, pd_r, pe_r,
    x_send, x_recv, pw_send, pw_recv, s1a_send, s1a_recv, s2a_send, s2a_recv, g_send, g_recv,
    s1b_send, s1b_recv, s2b_send, s2b_recv, wx_send, wx_recv, dx_send, dx_recv, sig_sem, w_sem, home_sem,
):
    nb, high, _, _, rows, width2 = w_in.shape
    width = width2 // 2
    nt = sig.shape[3]
    nh = nb // 2
    total = 4 * high * rows
    half = total // 2
    quarter = total // 4
    eighth = total // 8
    chunk = half // CHUNKS
    frames = nt * group
    bins = nb * bin_group
    me = lax.axis_index("frame")
    mb = lax.axis_index("bin")
    y = lax.rem(me, 2)
    lo = lax.rem(me // 2, 2)
    hi = me // 4
    near = high // 2
    hib = hi // near
    hir = lax.rem(hi, near)
    core = lax.rem(mb, 2)
    core_o = 1 - core
    y_dev = {"frame": me + 1 - 2 * y}
    lo_dev = {"frame": me + 2 - 4 * lo}
    core_dev = {"bin": mb + 1 - 2 * core}
    x_dev = {"bin": lax.rem(mb + 2, bin_group)}
    both_dev = {"bin": lax.rem(mb + 2, bin_group), "frame": me + 2 - 4 * lo}
    peers = [{"frame": lax.rem(hi + k, high) * 4 + lax.rem(me, 4)} for k in range(1, high)]

    def remote(a, b, s, r, dev):
        return pltpu.make_async_remote_copy(
            src_ref=a, dst_ref=b, send_sem=s, recv_sem=r, device_id=dev, device_id_type=MESH
        )

    def many(ref, sem):
        return pltpu.make_async_copy(ref, ref, sem)

    def x_copy(j, p):
        deep = 2 * sig.shape[2] // PIECES
        ref = lambda a: a.at[j, p // 2, pl.ds(pl.multiple_of(lax.rem(p, 2) * deep, deep), deep)]
        return remote(ref(xs), ref(xr), x_send.at[j, p], x_recv.at[j, p], lo_dev)

    def load_sig(f):
        return pltpu.make_async_copy(sig_hbm.at[f], sig.at[f], sig_sem.at[f])

    def load_w(f):
        return pltpu.make_async_copy(w_hbm.at[f], w_in.at[f], w_sem.at[f])

    def widen(j):
        f = (1 - lo) * nh + j
        load_sig(f).wait()
        xs[j] = sig[f].astype(f32)

    for j in range(nh):
        load_sig((1 - lo) * nh + j).start()
    barrier = pltpu.get_barrier_semaphore()
    for dev in [y_dev, lo_dev, core_dev, x_dev, both_dev] + peers:
        pl.semaphore_signal(barrier, inc=1, device_id=dev, device_id_type=MESH)
    for j in range(nh):
        load_sig(lo * nh + j).start()
        load_w(lo * nh + j).start()
        load_w((1 - lo) * nh + j).start()
    power[...] = jnp.zeros_like(power)
    for j in range(nh):
        widen(j)
    pl.semaphore_wait(barrier, 5 + len(peers))
    for n in range(EARLY):
        x_copy(n // PIECES, n % PIECES).start()

    def permute(f, to):
        for yd in range(2):
            for hd in range(high):
                for ld in range(2):
                    q = yd * 2 * high + hd // near * 2 * near + ld * near + hd % near
                    to[q * rows:(q + 1) * rows, :] = w_in[f, hd, ld, yd]

    def times(wr, wi, xr_, xi_):
        return dot(wr, xr_) - dot(wi, xi_), dot(wr, xi_) + dot(wi, xr_)

    def keep(j, b, yr, yi):
        src[j, b, 0] = yr
        src[j, b, 1] = yi
        yb[j, b, 0] = yr.astype(bf16)
        yb[j, b, 1] = yi.astype(bf16)

    def split(j, w):
        big = w.astype(bf16)
        w_hi[j] = big
        w_lo[j] = (w - big.astype(f32)).astype(bf16)

    def first(j, carry):
        f = lo * nh + j
        load_sig(f).wait()
        load_w(f).wait()
        load_w((1 - lo) * nh + j).wait()
        permute(f, flat.at[j])
        split(j, flat[j])
        yr, yi = times(w_hi[j, :, :width], w_hi[j, :, width:], sig[f, 0], sig[f, 1])
        keep(j, lo, yr, yi)
        power[0, lo] += yr * yr + yi * yi
        f = (1 - lo) * nh + j
        permute(f, tmp)
        wr, wi = tmp[:, :width].astype(bf16), tmp[:, width:].astype(bf16)
        yr, yi = times(wr, wi, sig[f, 0], sig[f, 1])
        power[0, lo] += yr * yr + yi * yi
        return carry

    lax.fori_loop(0, nh, first, 0)

    def piece(k, who):
        return pl.ds(pl.multiple_of(who * half + ORDER[k] * chunk, chunk), chunk)

    def pw(it, k, step, block):
        sems = pw_send.at[it, k, step], pw_recv.at[it, k, step]
        if step == 0:
            if it == 0:
                return remote(power.at[0, block, piece(k, core_o)], pa_r.at[0, k, block], *sems, core_dev)
            return remote(power.at[1, :, piece(k, core_o)], pa_r.at[1, k], *sems, core_dev)
        if step == 3:
            return remote(pd_s.at[it, k], pd_r.at[it, k], *sems, core_dev)
        if it == 0:
            a, b, dev = (pb_s, pb_r, x_dev) if step == 1 else (pc_s, pc_r, lo_dev)
            return remote(a.at[0, k, block], b.at[0, k, block], *sems, dev)
        b, dev = {1: (pb_r, x_dev), 2: (pc_r, lo_dev), 4: (pe_r, both_dev)}[step]
        return remote(pb_s.at[1, k], b.at[1, k], *sems, dev)

    def pw_a(it, k):
        pw(it, k, 0, lo).start()

    def pw_b(it, k):
        pw(it, k, 0, lo).wait()
        if it == 0:
            pb_s[0, k, lo] = power[0, lo, piece(k, core), :] + pa_r[0, k, lo]
        else:
            for b in range(2):
                pb_s[1, k, b] = power[1, b, piece(k, core), :] + pa_r[1, k, b]
        pw(it, k, 1, lo).start()
        if it == 1:
            pw(it, k, 2, lo).start()
            pw(it, k, 4, lo).start()

    def pw_c(k):
        pw(0, k, 1, lo).wait()
        pc_s[0, k, lo] = pb_s[0, k, lo] + pb_r[0, k, lo]
        pw(0, k, 2, lo).start()

    def inverse(p):
        return 1.0 / jnp.sqrt(p / bins + small_eps)

    def pw_d(it, k):
        if it == 0:
            pw(it, k, 2, lo).wait_send()
            pw(it, k, 2, 1 - lo).wait_recv()
            pd_s[0, k, lo] = pc_s[0, k, lo]
            pd_s[0, k, 1 - lo] = pc_r[0, k, 1 - lo]
        else:
            for step in (1, 2, 4):
                pw(it, k, step, lo).wait()
            pd_s[1, k] = (pb_s[1, k] + pb_r[1, k]) + (pc_r[1, k] + pe_r[1, k])
        pw(it, k, 3, lo).start()
        for b in range(2):
            rinv[b, piece(k, core), :] = inverse(pd_s[it, k, b])

    def pw_e(it, k):
        pw(it, k, 3, lo).wait()
        for b in range(2):
            rinv[b, piece(k, core_o), :] = inverse(pd_r[it, k, b])

    for k in range(4):
        pw_a(0, k)
    for k in range(4):
        pw_b(0, k)
    for k in range(4):
        pw_c(k)
    for n in range(EARLY, AHEAD):
        x_copy(n // PIECES, n % PIECES).start()
    for k in range(4):
        pw_d(0, k)
    for k in range(4):
        pw_e(0, k)

    def grams(j, slices):
        real = imag = None
        for b in range(2):
            scored = []
            for i in range(2):
                parts = [(src[j, b, i, its, :] * rinv[b, its, :]).astype(bf16) for its in slices]
                scored.append(jnp.concatenate(parts, axis=0) if len(parts) > 1 else parts[0])
            pr, pi = scored
            br, bi = yb[j, b, 0], yb[j, b, 1]
            re = dot_nt(pr, br) + dot_nt(pi, bi)
            im = dot_nt(pi, br) - dot_nt(pr, bi)
            real, imag = (re, im) if b == 0 else (real + re, imag + im)
        return real, imag

    def triple(acc, m_hi, m_lo):
        n = acc.shape[0]
        both = jnp.concatenate([acc[:, :width], acc[:, width:]], axis=0)
        big = both.astype(bf16)
        small = (both - big.astype(f32)).astype(bf16)
        out = dot(big, m_hi[...]) + (dot(small, m_hi[...]) + dot(big, m_lo[...]))
        a, b = out[:n], out[n:]
        return a[:, :width] - b[:, width:], a[:, width:] + b[:, :width]

    def at(c):
        return pl.ds(pl.multiple_of(c * chunk, chunk), chunk)

    def at_own(c):
        return pl.ds(pl.multiple_of(y * half + c * chunk, chunk), chunk)

    def at_other(c):
        return pl.ds(pl.multiple_of((1 - y) * half + c * chunk, chunk), chunk)

    def s1a(j, c):
        return remote(gram.at[j, 1 - y, at(c)], r1.at[j, at(c)], s1a_send.at[j, c], s1a_recv.at[j, c], y_dev)

    def s2a(j, c, k):
        return remote(part.at[j, at(c)], r2a.at[j, c, k - 1], s2a_send.at[j, c], s2a_recv.at[j, c], peers[k - 1])

    def g(j, its_rows, c):
        ref = w_next.at[j, its_rows]
        return remote(ref, ref, g_send.at[j, c], g_recv.at[j, c], y_dev)

    def arrive(j):
        for p in range(PIECES):
            x_copy(j, p).wait_recv()
        xb[j] = xr[j].astype(bf16)
        yr, yi = times(w_hi[j, :, :width], w_hi[j, :, width:], xb[j, 0], xb[j, 1])
        keep(j, 1 - lo, yr, yi)
        for away in range(2):
            h = y if away else 1 - y
            real, imag = grams(j, [pl.ds(pl.multiple_of(h * half, half), half)])
            gram[j, h, :, :width] = real
            gram[j, h, :, width:] = imag
            if away == 0:
                for c in ORDER:
                    s1a(j, c).start()

    def sum1(j, t, c):
        s1a(j, c).wait_recv()
        part[j, at(c)] = gram[j, y, at(c)] + r1[j, at(c)]
        for k in range(1, high):
            s2a(j, c, k).start()
        n = j * CHUNKS + t + AHEAD
        pl.when(n < nh * PIECES)(lambda: x_copy(n // PIECES, lax.rem(n, PIECES)).start())

    def update(j, t, c):
        many(r2a.at[j, c], s2a_recv.at[j, c]).wait()
        acc = part[j, at(c)]
        for k in range(high - 1):
            acc = acc + r2a[j, c, k]
        ar, ai = triple(acc * (1.0 / frames), w_hi.at[j], w_lo.at[j])
        w = flat[j, at_own(c)]
        wr, wi = w[:, :width], w[:, width:]
        w_next[j, at_own(c), :width] = wr + step_size * (wr - ar)
        w_next[j, at_own(c), width:] = wi + step_size * (wi - ai)
        g(j, at_own(c), c).start()

    def wx(j, from_lo):
        return remote(own.at[j, 1 - lo], w_out.at[from_lo * nh + j], wx_send.at[j], wx_recv.at[j], lo_dev)

    def w_home(j):
        return pltpu.make_async_copy(own.at[j, lo], w_out.at[lo * nh + j], home_sem.at[0, j])

    def p_home(j):
        return pltpu.make_async_copy(kept.at[j], p_out.at[lo * nh + j], home_sem.at[1, j])

    def mine(j):
        start = pl.multiple_of(y * half + hib * quarter, quarter)
        w = w_next[j, pl.ds(start, quarter), :]
        for l in range(2):
            for r in range(near):
                q = l * near + r
                if near == 1:
                    own[j, l] = w[q * rows:(q + 1) * rows]
                else:
                    pl.when(hir == r)(functools.partial(place, j, l, w[q * rows:(q + 1) * rows]))
        wx(j, lo).start()
        w_home(j).start()

    def place(j, l, w):
        own[j, l] = w

    def second(j, t, c):
        g(j, at_other(c), c).wait_recv()
        both = [at(c), pl.ds(pl.multiple_of(half + c * chunk, chunk), chunk)]
        w = jnp.concatenate([w_next[j, its] for its in both], axis=0)
        big = w.astype(bf16)
        small = (w - big.astype(f32)).astype(bf16)
        for h, its in enumerate(both):
            v_hi[j, its] = big[h * chunk:(h + 1) * chunk]
            v_lo[j, its] = small[h * chunk:(h + 1) * chunk]
        for b in range(2):
            x = (sig[lo * nh + j, 0], sig[lo * nh + j, 1]) if b == 0 else (xb[j, 0], xb[j, 1])
            yr, yi = times(big[:, :width], big[:, width:], *x)
            block = lo if b == 0 else 1 - lo
            squares = yr * yr + yi * yi
            for h, its in enumerate(both):
                here = slice(h * chunk, (h + 1) * chunk)
                src[j, block, 0, its] = yr[here]
                src[j, block, 1, its] = yi[here]
                yb[j, block, 0, its] = yr[here].astype(bf16)
                yb[j, block, 1, its] = yi[here].astype(bf16)
                power[1, block, its] += squares[here]

    units = nh * CHUNKS

    def stage_of(u):
        j, t = u // CHUNKS, lax.rem(u, CHUNKS)
        return j, t, lax.rem(t, 2) * 2 + t // 2

    def pipeline(s, carry):
        def on(lag, stage):
            u = s - lag
            pl.when(jnp.logical_and(u >= 0, u < units))(lambda: stage(*stage_of(u)))

        on(LAGS[0], sum1)
        on(LAGS[1], update)
        on(0, lambda j, t, c: pl.when(t == 0)(lambda: arrive(j)))
        on(LAGS[2], second)
        on(LAGS[2], lambda j, t, c: pl.when(t == CHUNKS - 1)(lambda: mine(j)))
        return carry

    lax.fori_loop(0, units, pipeline, 0)

    def run(stage, u):
        j, t = u // CHUNKS, u % CHUNKS
        stage(j, t, ORDER[t])

    for u in range(units - LAGS[0], units):
        run(sum1, u)
    tail = units - CHUNKS
    for u in range(units - LAGS[1], tail):
        run(update, u)
    for u in range(units - LAGS[2], tail):
        run(second, u)
        if u % CHUNKS == CHUNKS - 1:
            mine(u // CHUNKS)
    run(update, tail)
    run(update, tail + 1)
    run(second, tail)
    pw_a(1, 0)
    run(update, tail + 2)
    pw_b(1, 0)
    run(second, tail + 1)
    pw_a(1, 1)
    run(update, tail + 3)
    pw_b(1, 1)
    run(second, tail + 2)
    pw_a(1, 2)
    pw_d(1, 0)
    pw_b(1, 2)
    pw_e(1, 0)
    run(second, tail + 3)
    pw_a(1, 3)
    pw_d(1, 1)
    pw_b(1, 3)
    pw_e(1, 1)

    def dx(j, from_lo):
        return remote(prod.at[j], p_out.at[from_lo * nh + j], dx_send.at[j], dx_recv.at[j], lo_dev)

    lead = nh // 2

    def step_of(p):
        m = (p + nh - lead) // nh
        inner = lax.rem(m, 2)
        j = lo * lax.rem(p, nh) + (1 - lo) * (p - lead * inner - nh * (m // 2))
        return j, lo * (p // nh) + (1 - lo) * inner

    def s1b(j, l, i):
        return remote(
            gram_b.at[j, l, 0, i], r1b.at[j, l, i], s1b_send.at[j, l, i], s1b_recv.at[j, l, i], y_dev
        )

    def s2b(j, l, k):
        target = lax.rem(hi + k, high)
        i = 1 - lax.rem(target // near + hib, 2)
        return remote(
            last.at[j, l, i, lax.rem(target, near)], r2b.at[j, l, k - 1],
            s2b_send.at[j, l], s2b_recv.at[j, l], peers[k - 1],
        )

    def make_gram(p):
        j, l = step_of(p)
        slices = []
        for h in (1 - y, y):
            for sub in (1 - hib, hib):
                slices.append(pl.ds(pl.multiple_of(h * half + sub * quarter + l * eighth, eighth), eighth))
        real, imag = grams(j, slices)
        for h in range(2):
            for i in range(2):
                q = h * 2 + i
                gram_b[j, l, h, i, :, :width] = real[q * eighth:(q + 1) * eighth]
                gram_b[j, l, h, i, :, width:] = imag[q * eighth:(q + 1) * eighth]
        s1b(j, l, 0).start()
        s1b(j, l, 1).start()

    def sum1b(j, l, i):
        s1b(j, l, i).wait_recv()
        value = gram_b[j, l, 1, i] + r1b[j, l, i]
        for r in range(near):
            last[j, l, i, r] = value[r * rows:(r + 1) * rows]
        for k in range(1, high):
            there = lax.rem(lax.rem(hi + k, high) // near + hib, 2) == 1 - i
            pl.when(there)(lambda k=k: s2b(j, l, k).start())

    def send_on(p):
        j, l = step_of(p)
        sum1b(j, l, 0)

    def finish(p):
        j, l = step_of(p)
        sum1b(j, l, 1)
        many(r2b.at[j, l], s2b_recv.at[j, l]).wait()
        acc = last[j, l, 1, hir]
        for k in range(high - 1):
            acc = acc + r2b[j, l, k]
        ar, ai = triple(acc * (1.0 / frames), v_hi.at[j], v_lo.at[j])

        @pl.when(l != lo)
        def _():
            prod[j, :, :width] = ar
            prod[j, :, width:] = ai
            dx(j, lo).start()

        @pl.when(l == lo)
        def _():
            kept[j, :, :width] = ar
            kept[j, :, width:] = ai
            p_home(j).start()

    def each(stage, start, stop):
        def body(p, carry):
            stage(p)
            return carry

        lax.fori_loop(start, stop, body, 0)

    steps = 2 * nh
    each(make_gram, 0, lead)
    mine(nh - 1)
    pw_d(1, 2)
    pw_e(1, 2)
    each(send_on, 0, 1)
    pw_d(1, 3)
    pw_e(1, 3)
    each(make_gram, lead, steps)

    def both(p):
        pl.when(p < steps)(lambda: send_on(p))
        finish(p - BEHIND)

    def drain_first(j):
        for p in range(PIECES):
            x_copy(j, p).wait_send()
        for c in range(CHUNKS):
            s1a(j, c).wait_send()
            many(r2a.at[j, c], s2a_send.at[j, c]).wait()
            g(j, at_own(c), c).wait_send()
        w_home(j).wait()
        wx(j, lo).wait_send()
        wx(j, 1 - lo).wait_recv()

    def drain(j):
        for l in range(2):
            for i in range(2):
                s1b(j, l, i).wait_send()
            many(r2b.at[j, l], s2b_send.at[j, l]).wait()
        p_home(j).wait()
        dx(j, lo).wait_send()
        dx(j, 1 - lo).wait_recv()

    each(send_on, 1, BEHIND)
    each(drain_first, 0, nh)
    each(both, BEHIND, steps + BEHIND)

    each(drain, 0, nh)


def on_device(signal, demix):
    group = lax.axis_size("frame")
    bin_group = lax.axis_size("bin")
    nb, _, sensors, nt = signal.shape
    total, width2 = demix.shape[1:]
    rows = total // group
    high = group // 4
    half = total // 2
    eighth = total // 8
    nh = nb // 2
    out = jax.ShapeDtypeStruct((nb, rows, width2), f32)
    dma = pltpu.SemaphoreType.DMA
    hbm = pl.BlockSpec(memory_space=pl.ANY)
    piece = pltpu.VMEM((ITERS, 4, 2, eighth, nt), f32)
    own, product = pl.pallas_call(
        functools.partial(kernel, group, bin_group),
        out_shape=(out, out),
        in_specs=[hbm, hbm],
        out_specs=(hbm, hbm),
        scratch_shapes=[
            pltpu.VMEM((nb, 2, sensors, nt), bf16),
            pltpu.VMEM((nb, high, 2, 2, rows, width2), f32),
            pltpu.VMEM((nh, 2, sensors, nt), f32),
            pltpu.VMEM((nh, 2, sensors, nt), f32),
            pltpu.VMEM((nh, 2, sensors, nt), bf16),
            pltpu.VMEM((total, width2), f32),
            pltpu.VMEM((nh, total, width2), f32),
            pltpu.VMEM((nh, total, width2), f32),
            pltpu.VMEM((nh, total, width2), bf16),
            pltpu.VMEM((nh, total, width2), bf16),
            pltpu.VMEM((nh, total, width2), bf16),
            pltpu.VMEM((nh, total, width2), bf16),
            pltpu.VMEM((nh, 2, 2, total, nt), f32),
            pltpu.VMEM((nh, 2, 2, total, nt), bf16),
            pltpu.VMEM((nh, 2, half, width2), f32),
            pltpu.VMEM((nh, half, width2), f32),
            pltpu.VMEM((nh, half, width2), f32),
            pltpu.VMEM((nh, CHUNKS, high - 1, half // CHUNKS, width2), f32),
            pltpu.VMEM((nh, 2, 2, 2, eighth, width2), f32),
            pltpu.VMEM((nh, 2, 2, eighth, width2), f32),
            pltpu.VMEM((nh, 2, 2, high // 2, rows, width2), f32),
            pltpu.VMEM((nh, 2, high - 1, rows, width2), f32),
            pltpu.VMEM((nh, 2, rows, width2), f32),
            pltpu.VMEM((nh, rows, width2), f32),
            pltpu.VMEM((nh, rows, width2), f32),
            pltpu.VMEM((ITERS, 2, total, nt), f32),
            pltpu.VMEM((2, total, nt), f32),
            piece, piece, piece, piece, piece, piece, piece, piece,
            dma((nh, PIECES)), dma((nh, PIECES)),
            dma((ITERS, 4, 5)), dma((ITERS, 4, 5)),
            dma((nh, CHUNKS)), dma((nh, CHUNKS)),
            dma((nh, CHUNKS)), dma((nh, CHUNKS)),
            dma((nh, CHUNKS)), dma((nh, CHUNKS)),
            dma((nh, 2, 2)), dma((nh, 2, 2)),
            dma((nh, 2)), dma((nh, 2)),
            dma((nh,)), dma((nh,)),
            dma((nh,)), dma((nh,)),
            dma((nb,)), dma((nb,)), dma((2, nh)),
        ],
        compiler_params=pltpu.CompilerParams(
            collective_id=0, has_side_effects=True, vmem_limit_bytes=62 * 1024 * 1024
        ),
    )(signal, demix.reshape(nb, high, 2, 2, rows, width2))
    direction = own - product
    return own + step_size * direction, direction


def solution(mesh):
    placed = (P("bin", None, None, "frame"), P("bin", None, None))
    return jax.shard_map(
        on_device,
        mesh=mesh,
        in_specs=placed,
        out_specs=(P("bin", "frame", None), P("bin", "frame", None)),
        check_vma=False,
    )
```

```python
import functools

import jax
import jax.numpy as jnp
from jax import lax
from jax.experimental import pallas as pl
from jax.experimental.pallas import tpu as pltpu
from jax.sharding import PartitionSpec as P

ITERS = 2
CHUNKS = 4
ORDER = (0, 2, 1, 3)
BEHIND = 2
LAGS = (1, 4, 6)
PIECES = 4
EARLY = 4
AHEAD = 9

step_size = 0.05
small_eps = 1e-06

MESH = pl.DeviceIdType.MESH
NT = (((1,), (1,)), ((), ()))
f32 = jnp.float32
bf16 = jnp.bfloat16


def dot(a, b):
    return jnp.dot(a, b, preferred_element_type=f32)


def dot_nt(a, b):
    return lax.dot_general(a, b, NT, preferred_element_type=f32)


def kernel(
    group, bin_group, sig_hbm, w_hbm, w_out, p_out,
    sig, w_in, xs, xr, xb, tmp, flat, w_next, w_hi, w_lo, v_hi, v_lo, src, yb,
    gram, r1, part, r2a, gram_b, r1b, last, r2b, own, prod, kept,
    power, rinv, pa_r, pb_s, pb_r, pc_s, pc_r, pd_s, pd_r, pe_r,
    x_send, x_recv, pw_send, pw_recv, s1a_send, s1a_recv, s2a_send, s2a_recv, g_send, g_recv,
    s1b_send, s1b_recv, s2b_send, s2b_recv, wx_send, wx_recv, dx_send, dx_recv, sig_sem, w_sem, home_sem,
):
    nb, high, _, _, rows, width2 = w_in.shape
    width = width2 // 2
    nt = sig.shape[3]
    nh = nb // 2
    total = 4 * high * rows
    half = total // 2
    quarter = total // 4
    eighth = total // 8
    chunk = half // CHUNKS
    frames = nt * group
    bins = nb * bin_group
    me = lax.axis_index("frame")
    mb = lax.axis_index("bin")
    y = lax.rem(me, 2)
    lo = lax.rem(me // 2, 2)
    hi = me // 4
    near = high // 2
    hib = hi // near
    hir = lax.rem(hi, near)
    core = lax.rem(mb, 2)
    core_o = 1 - core
    y_dev = {"frame": me + 1 - 2 * y}
    lo_dev = {"frame": me + 2 - 4 * lo}
    core_dev = {"bin": mb + 1 - 2 * core}
    x_dev = {"bin": lax.rem(mb + 2, bin_group)}
    both_dev = {"bin": lax.rem(mb + 2, bin_group), "frame": me + 2 - 4 * lo}
    peers = [{"frame": lax.rem(hi + k, high) * 4 + lax.rem(me, 4)} for k in range(1, high)]

    def remote(a, b, s, r, dev):
        return pltpu.make_async_remote_copy(
            src_ref=a, dst_ref=b, send_sem=s, recv_sem=r, device_id=dev, device_id_type=MESH
        )

    def many(ref, sem):
        return pltpu.make_async_copy(ref, ref, sem)

    def x_copy(j, p):
        deep = 2 * sig.shape[2] // PIECES
        ref = lambda a: a.at[j, p // 2, pl.ds(pl.multiple_of(lax.rem(p, 2) * deep, deep), deep)]
        return remote(ref(xs), ref(xr), x_send.at[j, p], x_recv.at[j, p], lo_dev)

    def load_sig(f):
        return pltpu.make_async_copy(sig_hbm.at[f], sig.at[f], sig_sem.at[f])

    def load_w(f):
        return pltpu.make_async_copy(w_hbm.at[f], w_in.at[f], w_sem.at[f])

    def widen(j):
        f = (1 - lo) * nh + j
        load_sig(f).wait()
        xs[j] = sig[f].astype(f32)

    for j in range(nh):
        load_sig((1 - lo) * nh + j).start()
    barrier = pltpu.get_barrier_semaphore()
    for dev in [y_dev, lo_dev, core_dev, x_dev, both_dev] + peers:
        pl.semaphore_signal(barrier, inc=1, device_id=dev, device_id_type=MESH)
    for j in range(nh):
        load_sig(lo * nh + j).start()
        load_w(lo * nh + j).start()
        load_w((1 - lo) * nh + j).start()
    power[...] = jnp.zeros_like(power)
    for j in range(nh):
        widen(j)
    pl.semaphore_wait(barrier, 5 + len(peers))
    for n in range(EARLY):
        x_copy(n // PIECES, n % PIECES).start()

    def permute(f, to):
        for yd in range(2):
            for hd in range(high):
                for ld in range(2):
                    q = yd * 2 * high + hd // near * 2 * near + ld * near + hd % near
                    to[q * rows:(q + 1) * rows, :] = w_in[f, hd, ld, yd]

    def times(wr, wi, xr_, xi_):
        return dot(wr, xr_) - dot(wi, xi_), dot(wr, xi_) + dot(wi, xr_)

    def keep(j, b, yr, yi):
        src[j, b, 0] = yr
        src[j, b, 1] = yi
        yb[j, b, 0] = yr.astype(bf16)
        yb[j, b, 1] = yi.astype(bf16)

    def split(j, w):
        big = w.astype(bf16)
        w_hi[j] = big
        w_lo[j] = (w - big.astype(f32)).astype(bf16)

    def first(j, carry):
        f = lo * nh + j
        load_sig(f).wait()
        load_w(f).wait()
        load_w((1 - lo) * nh + j).wait()
        permute(f, flat.at[j])
        split(j, flat[j])
        yr, yi = times(w_hi[j, :, :width], w_hi[j, :, width:], sig[f, 0], sig[f, 1])
        keep(j, lo, yr, yi)
        power[0, lo] += yr * yr + yi * yi
        f = (1 - lo) * nh + j
        permute(f, tmp)
        wr, wi = tmp[:, :width].astype(bf16), tmp[:, width:].astype(bf16)
        yr, yi = times(wr, wi, sig[f, 0], sig[f, 1])
        power[0, lo] += yr * yr + yi * yi
        return carry

    lax.fori_loop(0, nh, first, 0)

    def piece(k, who):
        return pl.ds(pl.multiple_of(who * half + ORDER[k] * chunk, chunk), chunk)

    def pw(it, k, step, block):
        sems = pw_send.at[it, k, step], pw_recv.at[it, k, step]
        if step == 0:
            if it == 0:
                return remote(power.at[0, block, piece(k, core_o)], pa_r.at[0, k, block], *sems, core_dev)
            return remote(power.at[1, :, piece(k, core_o)], pa_r.at[1, k], *sems, core_dev)
        if step == 3:
            return remote(pd_s.at[it, k], pd_r.at[it, k], *sems, core_dev)
        if it == 0:
            a, b, dev = (pb_s, pb_r, x_dev) if step == 1 else (pc_s, pc_r, lo_dev)
            return remote(a.at[0, k, block], b.at[0, k, block], *sems, dev)
        b, dev = {1: (pb_r, x_dev), 2: (pc_r, lo_dev), 4: (pe_r, both_dev)}[step]
        return remote(pb_s.at[1, k], b.at[1, k], *sems, dev)

    def pw_a(it, k):
        pw(it, k, 0, lo).start()

    def pw_b(it, k):
        pw(it, k, 0, lo).wait()
        if it == 0:
            pb_s[0, k, lo] = power[0, lo, piece(k, core), :] + pa_r[0, k, lo]
        else:
            for b in range(2):
                pb_s[1, k, b] = power[1, b, piece(k, core), :] + pa_r[1, k, b]
        pw(it, k, 1, lo).start()
        if it == 1:
            pw(it, k, 2, lo).start()
            pw(it, k, 4, lo).start()

    def pw_c(k):
        pw(0, k, 1, lo).wait()
        pc_s[0, k, lo] = pb_s[0, k, lo] + pb_r[0, k, lo]
        pw(0, k, 2, lo).start()

    def inverse(p):
        return 1.0 / jnp.sqrt(p / bins + small_eps)

    def pw_d(it, k):
        if it == 0:
            pw(it, k, 2, lo).wait_send()
            pw(it, k, 2, 1 - lo).wait_recv()
            pd_s[0, k, lo] = pc_s[0, k, lo]
            pd_s[0, k, 1 - lo] = pc_r[0, k, 1 - lo]
        else:
            for step in (1, 2, 4):
                pw(it, k, step, lo).wait()
            pd_s[1, k] = (pb_s[1, k] + pb_r[1, k]) + (pc_r[1, k] + pe_r[1, k])
        pw(it, k, 3, lo).start()
        for b in range(2):
            rinv[b, piece(k, core), :] = inverse(pd_s[it, k, b])

    def pw_e(it, k):
        pw(it, k, 3, lo).wait()
        for b in range(2):
            rinv[b, piece(k, core_o), :] = inverse(pd_r[it, k, b])

    for k in range(4):
        pw_a(0, k)
    for k in range(4):
        pw_b(0, k)
    for k in range(4):
        pw_c(k)
    for n in range(EARLY, AHEAD):
        x_copy(n // PIECES, n % PIECES).start()
    for k in range(4):
        pw_d(0, k)
    for k in range(4):
        pw_e(0, k)

    def grams(j, slices):
        real = imag = None
        for b in range(2):
            scored = []
            for i in range(2):
                parts = [(src[j, b, i, its, :] * rinv[b, its, :]).astype(bf16) for its in slices]
                scored.append(jnp.concatenate(parts, axis=0) if len(parts) > 1 else parts[0])
            pr, pi = scored
            br, bi = yb[j, b, 0], yb[j, b, 1]
            re = dot_nt(pr, br) + dot_nt(pi, bi)
            im = dot_nt(pi, br) - dot_nt(pr, bi)
            real, imag = (re, im) if b == 0 else (real + re, imag + im)
        return real, imag

    def triple(acc, m_hi, m_lo):
        n = acc.shape[0]
        both = jnp.concatenate([acc[:, :width], acc[:, width:]], axis=0)
        big = both.astype(bf16)
        small = (both - big.astype(f32)).astype(bf16)
        out = dot(big, m_hi[...]) + (dot(small, m_hi[...]) + dot(big, m_lo[...]))
        a, b = out[:n], out[n:]
        return a[:, :width] - b[:, width:], a[:, width:] + b[:, :width]

    def at(c):
        return pl.ds(pl.multiple_of(c * chunk, chunk), chunk)

    def at_own(c):
        return pl.ds(pl.multiple_of(y * half + c * chunk, chunk), chunk)

    def at_other(c):
        return pl.ds(pl.multiple_of((1 - y) * half + c * chunk, chunk), chunk)

    def s1a(j, c):
        return remote(gram.at[j, 1 - y, at(c)], r1.at[j, at(c)], s1a_send.at[j, c], s1a_recv.at[j, c], y_dev)

    def s2a(j, c, k):
        return remote(part.at[j, at(c)], r2a.at[j, c, k - 1], s2a_send.at[j, c], s2a_recv.at[j, c], peers[k - 1])

    def g(j, its_rows, c):
        ref = w_next.at[j, its_rows]
        return remote(ref, ref, g_send.at[j, c], g_recv.at[j, c], y_dev)

    def arrive(j):
        for p in range(PIECES):
            x_copy(j, p).wait_recv()
        xb[j] = xr[j].astype(bf16)
        yr, yi = times(w_hi[j, :, :width], w_hi[j, :, width:], xb[j, 0], xb[j, 1])
        keep(j, 1 - lo, yr, yi)
        for away in range(2):
            h = y if away else 1 - y
            real, imag = grams(j, [pl.ds(pl.multiple_of(h * half, half), half)])
            gram[j, h, :, :width] = real
            gram[j, h, :, width:] = imag
            if away == 0:
                for c in ORDER:
                    s1a(j, c).start()

    def sum1(j, t, c):
        s1a(j, c).wait_recv()
        part[j, at(c)] = gram[j, y, at(c)] + r1[j, at(c)]
        for k in range(1, high):
            s2a(j, c, k).start()
        n = j * CHUNKS + t + AHEAD
        pl.when(n < nh * PIECES)(lambda: x_copy(n // PIECES, lax.rem(n, PIECES)).start())

    def update(j, t, c):
        many(r2a.at[j, c], s2a_recv.at[j, c]).wait()
        acc = part[j, at(c)]
        for k in range(high - 1):
            acc = acc + r2a[j, c, k]
        ar, ai = triple(acc * (1.0 / frames), w_hi.at[j], w_lo.at[j])
        w = flat[j, at_own(c)]
        wr, wi = w[:, :width], w[:, width:]
        w_next[j, at_own(c), :width] = wr + step_size * (wr - ar)
        w_next[j, at_own(c), width:] = wi + step_size * (wi - ai)
        g(j, at_own(c), c).start()

    def wx(j, from_lo):
        return remote(own.at[j, 1 - lo], w_out.at[from_lo * nh + j], wx_send.at[j], wx_recv.at[j], lo_dev)

    def w_home(j):
        return pltpu.make_async_copy(own.at[j, lo], w_out.at[lo * nh + j], home_sem.at[0, j])

    def p_home(j):
        return pltpu.make_async_copy(kept.at[j], p_out.at[lo * nh + j], home_sem.at[1, j])

    def mine(j):
        start = pl.multiple_of(y * half + hib * quarter, quarter)
        w = w_next[j, pl.ds(start, quarter), :]
        for l in range(2):
            for r in range(near):
                q = l * near + r
                if near == 1:
                    own[j, l] = w[q * rows:(q + 1) * rows]
                else:
                    pl.when(hir == r)(functools.partial(place, j, l, w[q * rows:(q + 1) * rows]))
        wx(j, lo).start()
        w_home(j).start()

    def place(j, l, w):
        own[j, l] = w

    def second(j, t, c):
        g(j, at_other(c), c).wait_recv()
        both = [at(c), pl.ds(pl.multiple_of(half + c * chunk, chunk), chunk)]
        w = jnp.concatenate([w_next[j, its] for its in both], axis=0)
        big = w.astype(bf16)
        small = (w - big.astype(f32)).astype(bf16)
        for h, its in enumerate(both):
            v_hi[j, its] = big[h * chunk:(h + 1) * chunk]
            v_lo[j, its] = small[h * chunk:(h + 1) * chunk]
        for b in range(2):
            x = (sig[lo * nh + j, 0], sig[lo * nh + j, 1]) if b == 0 else (xb[j, 0], xb[j, 1])
            yr, yi = times(big[:, :width], big[:, width:], *x)
            block = lo if b == 0 else 1 - lo
            squares = yr * yr + yi * yi
            for h, its in enumerate(both):
                here = slice(h * chunk, (h + 1) * chunk)
                src[j, block, 0, its] = yr[here]
                src[j, block, 1, its] = yi[here]
                yb[j, block, 0, its] = yr[here].astype(bf16)
                yb[j, block, 1, its] = yi[here].astype(bf16)
                power[1, block, its] += squares[here]

    units = nh * CHUNKS

    def stage_of(u):
        j, t = u // CHUNKS, lax.rem(u, CHUNKS)
        return j, t, lax.rem(t, 2) * 2 + t // 2

    def pipeline(s, carry):
        def on(lag, stage):
            u = s - lag
            pl.when(jnp.logical_and(u >= 0, u < units))(lambda: stage(*stage_of(u)))

        on(LAGS[0], sum1)
        on(LAGS[1], update)
        on(0, lambda j, t, c: pl.when(t == 0)(lambda: arrive(j)))
        on(LAGS[2], second)
        on(LAGS[2], lambda j, t, c: pl.when(t == CHUNKS - 1)(lambda: mine(j)))
        return carry

    lax.fori_loop(0, units, pipeline, 0)

    def run(stage, u):
        j, t = u // CHUNKS, u % CHUNKS
        stage(j, t, ORDER[t])

    for u in range(units - LAGS[0], units):
        run(sum1, u)
    tail = units - CHUNKS
    for u in range(units - LAGS[1], tail):
        run(update, u)
    for u in range(units - LAGS[2], tail):
        run(second, u)
        if u % CHUNKS == CHUNKS - 1:
            mine(u // CHUNKS)
    run(update, tail)
    run(update, tail + 1)
    run(second, tail)
    pw_a(1, 0)
    run(update, tail + 2)
    pw_b(1, 0)
    run(second, tail + 1)
    pw_a(1, 1)
    run(update, tail + 3)
    pw_b(1, 1)
    run(second, tail + 2)
    pw_a(1, 2)
    pw_d(1, 0)
    pw_b(1, 2)
    pw_e(1, 0)
    run(second, tail + 3)
    pw_a(1, 3)
    pw_d(1, 1)
    pw_b(1, 3)
    pw_e(1, 1)

    def dx(j, from_lo):
        return remote(prod.at[j], p_out.at[from_lo * nh + j], dx_send.at[j], dx_recv.at[j], lo_dev)

    lead = nh // 2

    def step_of(p):
        m = (p + nh - lead) // nh
        inner = lax.rem(m, 2)
        j = lo * lax.rem(p, nh) + (1 - lo) * (p - lead * inner - nh * (m // 2))
        return j, lo * (p // nh) + (1 - lo) * inner

    def s1b(j, l, i):
        return remote(
            gram_b.at[j, l, 0, i], r1b.at[j, l, i], s1b_send.at[j, l, i], s1b_recv.at[j, l, i], y_dev
        )

    def s2b(j, l, k):
        target = lax.rem(hi + k, high)
        i = 1 - lax.rem(target // near + hib, 2)
        return remote(
            last.at[j, l, i, lax.rem(target, near)], r2b.at[j, l, k - 1],
            s2b_send.at[j, l], s2b_recv.at[j, l], peers[k - 1],
        )

    def make_gram(p):
        j, l = step_of(p)
        slices = []
        for h in (1 - y, y):
            for sub in (1 - hib, hib):
                slices.append(pl.ds(pl.multiple_of(h * half + sub * quarter + l * eighth, eighth), eighth))
        real, imag = grams(j, slices)
        for h in range(2):
            for i in range(2):
                q = h * 2 + i
                gram_b[j, l, h, i, :, :width] = real[q * eighth:(q + 1) * eighth]
                gram_b[j, l, h, i, :, width:] = imag[q * eighth:(q + 1) * eighth]
        s1b(j, l, 0).start()
        s1b(j, l, 1).start()

    def sum1b(j, l, i):
        s1b(j, l, i).wait_recv()
        value = gram_b[j, l, 1, i] + r1b[j, l, i]
        for r in range(near):
            last[j, l, i, r] = value[r * rows:(r + 1) * rows]
        for k in range(1, high):
            there = lax.rem(lax.rem(hi + k, high) // near + hib, 2) == 1 - i
            pl.when(there)(lambda k=k: s2b(j, l, k).start())

    def send_on(p):
        j, l = step_of(p)
        sum1b(j, l, 0)

    def finish(p):
        j, l = step_of(p)
        sum1b(j, l, 1)
        many(r2b.at[j, l], s2b_recv.at[j, l]).wait()
        acc = last[j, l, 1, hir]
        for k in range(high - 1):
            acc = acc + r2b[j, l, k]
        ar, ai = triple(acc * (1.0 / frames), v_hi.at[j], v_lo.at[j])

        @pl.when(l != lo)
        def _():
            prod[j, :, :width] = ar
            prod[j, :, width:] = ai
            dx(j, lo).start()

        @pl.when(l == lo)
        def _():
            kept[j, :, :width] = ar
            kept[j, :, width:] = ai
            p_home(j).start()

    def each(stage, start, stop):
        def body(p, carry):
            stage(p)
            return carry

        lax.fori_loop(start, stop, body, 0)

    steps = 2 * nh
    each(make_gram, 0, lead)
    mine(nh - 1)
    pw_d(1, 2)
    pw_e(1, 2)
    each(send_on, 0, 1)
    pw_d(1, 3)
    pw_e(1, 3)
    each(make_gram, lead, steps)

    def both(p):
        pl.when(p < steps)(lambda: send_on(p))
        finish(p - BEHIND)

    def drain_first(j):
        for p in range(PIECES):
            x_copy(j, p).wait_send()
        for c in range(CHUNKS):
            s1a(j, c).wait_send()
            many(r2a.at[j, c], s2a_send.at[j, c]).wait()
            g(j, at_own(c), c).wait_send()
        w_home(j).wait()
        wx(j, lo).wait_send()
        wx(j, 1 - lo).wait_recv()

    def drain(j):
        for l in range(2):
            for i in range(2):
                s1b(j, l, i).wait_send()
            many(r2b.at[j, l], s2b_send.at[j, l]).wait()
        p_home(j).wait()
        dx(j, lo).wait_send()
        dx(j, 1 - lo).wait_recv()

    each(send_on, 1, BEHIND)
    each(drain_first, 0, nh)
    each(both, BEHIND, steps + BEHIND)

    each(drain, 0, nh)


def on_device(signal, demix):
    group = lax.axis_size("frame")
    bin_group = lax.axis_size("bin")
    nb, _, sensors, nt = signal.shape
    total, width2 = demix.shape[1:]
    rows = total // group
    high = group // 4
    half = total // 2
    eighth = total // 8
    nh = nb // 2
    out = jax.ShapeDtypeStruct((nb, rows, width2), f32)
    dma = pltpu.SemaphoreType.DMA
    hbm = pl.BlockSpec(memory_space=pl.ANY)
    piece = pltpu.VMEM((ITERS, 4, 2, eighth, nt), f32)
    own, product = pl.pallas_call(
        functools.partial(kernel, group, bin_group),
        out_shape=(out, out),
        in_specs=[hbm, hbm],
        out_specs=(hbm, hbm),
        scratch_shapes=[
            pltpu.VMEM((nb, 2, sensors, nt), bf16),
            pltpu.VMEM((nb, high, 2, 2, rows, width2), f32),
            pltpu.VMEM((nh, 2, sensors, nt), f32),
            pltpu.VMEM((nh, 2, sensors, nt), f32),
            pltpu.VMEM((nh, 2, sensors, nt), bf16),
            pltpu.VMEM((total, width2), f32),
            pltpu.VMEM((nh, total, width2), f32),
            pltpu.VMEM((nh, total, width2), f32),
            pltpu.VMEM((nh, total, width2), bf16),
            pltpu.VMEM((nh, total, width2), bf16),
            pltpu.VMEM((nh, total, width2), bf16),
            pltpu.VMEM((nh, total, width2), bf16),
            pltpu.VMEM((nh, 2, 2, total, nt), f32),
            pltpu.VMEM((nh, 2, 2, total, nt), bf16),
            pltpu.VMEM((nh, 2, half, width2), f32),
            pltpu.VMEM((nh, half, width2), f32),
            pltpu.VMEM((nh, half, width2), f32),
            pltpu.VMEM((nh, CHUNKS, high - 1, half // CHUNKS, width2), f32),
            pltpu.VMEM((nh, 2, 2, 2, eighth, width2), f32),
            pltpu.VMEM((nh, 2, 2, eighth, width2), f32),
            pltpu.VMEM((nh, 2, 2, high // 2, rows, width2), f32),
            pltpu.VMEM((nh, 2, high - 1, rows, width2), f32),
            pltpu.VMEM((nh, 2, rows, width2), f32),
            pltpu.VMEM((nh, rows, width2), f32),
            pltpu.VMEM((nh, rows, width2), f32),
            pltpu.VMEM((ITERS, 2, total, nt), f32),
            pltpu.VMEM((2, total, nt), f32),
            piece, piece, piece, piece, piece, piece, piece, piece,
            dma((nh, PIECES)), dma((nh, PIECES)),
            dma((ITERS, 4, 5)), dma((ITERS, 4, 5)),
            dma((nh, CHUNKS)), dma((nh, CHUNKS)),
            dma((nh, CHUNKS)), dma((nh, CHUNKS)),
            dma((nh, CHUNKS)), dma((nh, CHUNKS)),
            dma((nh, 2, 2)), dma((nh, 2, 2)),
            dma((nh, 2)), dma((nh, 2)),
            dma((nh,)), dma((nh,)),
            dma((nh,)), dma((nh,)),
            dma((nb,)), dma((nb,)), dma((2, nh)),
        ],
        compiler_params=pltpu.CompilerParams(
            collective_id=0, has_side_effects=True, vmem_limit_bytes=(51 if high == 2 else 62) * 1024 * 1024
        ),
    )(signal, demix.reshape(nb, high, 2, 2, rows, width2))
    direction = own - product
    return own + step_size * direction, direction


def solution(mesh):
    placed = (P("bin", None, None, "frame"), P("bin", None, None))
    return jax.shard_map(
        on_device,
        mesh=mesh,
        in_specs=placed,
        out_specs=(P("bin", "frame", None), P("bin", "frame", None)),
        check_vma=False,
    )
```

```python
import functools

import jax
import jax.numpy as jnp
from jax import lax
from jax.experimental import pallas as pl
from jax.experimental.pallas import tpu as pltpu
from jax.sharding import PartitionSpec as P

ITERS = 2
CHUNKS = 4
ORDER = (0, 2, 1, 3)
BEHIND = 2
LAGS = (1, 4, 6)
PIECES = 4
EARLY = 4
AHEAD = 9

step_size = 0.05
small_eps = 1e-06

MESH = pl.DeviceIdType.MESH
NT = (((1,), (1,)), ((), ()))
f32 = jnp.float32
bf16 = jnp.bfloat16


def dot(a, b):
    return jnp.dot(a, b, preferred_element_type=f32)


def dot_nt(a, b):
    return lax.dot_general(a, b, NT, preferred_element_type=f32)


def kernel(
    group, bin_group, sig_hbm, w_hbm, w_out, p_out,
    sig, w_in, xs, xr, xb, tmp, flat, w_next, w_hi, w_lo, v_hi, v_lo, src, yb,
    gram, r1, part, r2a, gram_b, r1b, last, r2b, own, prod, kept,
    power, rinv, pa_r, pb_s, pb_r, pc_s, pc_r, pd_s, pd_r, pe_r,
    x_send, x_recv, pw_send, pw_recv, s1a_send, s1a_recv, s2a_send, s2a_recv, g_send, g_recv,
    s1b_send, s1b_recv, s2b_send, s2b_recv, wx_send, wx_recv, dx_send, dx_recv, sig_sem, w_sem, home_sem,
):
    nb, high, _, _, rows, width2 = w_in.shape
    width = width2 // 2
    nt = sig.shape[3]
    nh = nb // 2
    total = 4 * high * rows
    half = total // 2
    quarter = total // 4
    eighth = total // 8
    chunk = half // CHUNKS
    frames = nt * group
    bins = nb * bin_group
    me = lax.axis_index("frame")
    mb = lax.axis_index("bin")
    y = lax.rem(me, 2)
    lo = lax.rem(me // 2, 2)
    hi = me // 4
    near = high // 2
    hib = hi // near
    hir = lax.rem(hi, near)
    core = lax.rem(mb, 2)
    core_o = 1 - core
    y_dev = {"frame": me + 1 - 2 * y}
    lo_dev = {"frame": me + 2 - 4 * lo}
    core_dev = {"bin": mb + 1 - 2 * core}
    x_dev = {"bin": lax.rem(mb + 2, bin_group)}
    both_dev = {"bin": lax.rem(mb + 2, bin_group), "frame": me + 2 - 4 * lo}
    peers = [{"frame": lax.rem(hi + k, high) * 4 + lax.rem(me, 4)} for k in range(1, high)]

    def remote(a, b, s, r, dev):
        return pltpu.make_async_remote_copy(
            src_ref=a, dst_ref=b, send_sem=s, recv_sem=r, device_id=dev, device_id_type=MESH
        )

    def many(ref, sem):
        return pltpu.make_async_copy(ref, ref, sem)

    def x_copy(j, p):
        deep = 2 * sig.shape[2] // PIECES
        ref = lambda a: a.at[j, p // 2, pl.ds(pl.multiple_of(lax.rem(p, 2) * deep, deep), deep)]
        return remote(ref(xs), ref(xr), x_send.at[j, p], x_recv.at[j, p], lo_dev)

    def load_sig(f):
        return pltpu.make_async_copy(sig_hbm.at[f], sig.at[f], sig_sem.at[f])

    def load_w(f):
        return pltpu.make_async_copy(w_hbm.at[f], w_in.at[f], w_sem.at[f])

    def widen(j):
        f = (1 - lo) * nh + j
        load_sig(f).wait()
        xs[j] = sig[f].astype(f32)

    for j in range(nh):
        load_sig((1 - lo) * nh + j).start()
    barrier = pltpu.get_barrier_semaphore()
    for dev in [y_dev, lo_dev, core_dev, x_dev, both_dev] + peers:
        pl.semaphore_signal(barrier, inc=1, device_id=dev, device_id_type=MESH)
    for j in range(nh):
        load_sig(lo * nh + j).start()
        load_w(lo * nh + j).start()
        load_w((1 - lo) * nh + j).start()
    power[...] = jnp.zeros_like(power)
    for j in range(nh):
        widen(j)
    pl.semaphore_wait(barrier, 5 + len(peers))
    for n in range(EARLY):
        x_copy(n // PIECES, n % PIECES).start()

    def permute(f, to):
        for yd in range(2):
            for hd in range(high):
                for ld in range(2):
                    q = yd * 2 * high + hd // near * 2 * near + ld * near + hd % near
                    to[q * rows:(q + 1) * rows, :] = w_in[f, hd, ld, yd]

    def times(wr, wi, xr_, xi_):
        return dot(wr, xr_) - dot(wi, xi_), dot(wr, xi_) + dot(wi, xr_)

    def keep(j, b, yr, yi):
        src[j, b, 0] = yr
        src[j, b, 1] = yi
        yb[j, b, 0] = yr.astype(bf16)
        yb[j, b, 1] = yi.astype(bf16)

    def split(j, w):
        big = w.astype(bf16)
        w_hi[j] = big
        w_lo[j] = (w - big.astype(f32)).astype(bf16)

    def first(j, carry):
        f = lo * nh + j
        load_sig(f).wait()
        load_w(f).wait()
        load_w((1 - lo) * nh + j).wait()
        permute(f, flat.at[j])
        split(j, flat[j])
        yr, yi = times(w_hi[j, :, :width], w_hi[j, :, width:], sig[f, 0], sig[f, 1])
        keep(j, lo, yr, yi)
        power[0, lo] += yr * yr + yi * yi
        f = (1 - lo) * nh + j
        permute(f, tmp)
        wr, wi = tmp[:, :width].astype(bf16), tmp[:, width:].astype(bf16)
        yr, yi = times(wr, wi, sig[f, 0], sig[f, 1])
        power[0, lo] += yr * yr + yi * yi
        return carry

    lax.fori_loop(0, nh, first, 0)

    def piece(k, who):
        return pl.ds(pl.multiple_of(who * half + ORDER[k] * chunk, chunk), chunk)

    def pw(it, k, step, block):
        sems = pw_send.at[it, k, step], pw_recv.at[it, k, step]
        if step == 0:
            if it == 0:
                return remote(power.at[0, block, piece(k, core_o)], pa_r.at[0, k, block], *sems, core_dev)
            return remote(power.at[1, :, piece(k, core_o)], pa_r.at[1, k], *sems, core_dev)
        if step == 3:
            return remote(pd_s.at[it, k], pd_r.at[it, k], *sems, core_dev)
        if it == 0:
            a, b, dev = (pb_s, pb_r, x_dev) if step == 1 else (pc_s, pc_r, lo_dev)
            return remote(a.at[0, k, block], b.at[0, k, block], *sems, dev)
        b, dev = {1: (pb_r, x_dev), 2: (pc_r, lo_dev), 4: (pe_r, both_dev)}[step]
        return remote(pb_s.at[1, k], b.at[1, k], *sems, dev)

    def pw_a(it, k):
        pw(it, k, 0, lo).start()

    def pw_b(it, k):
        pw(it, k, 0, lo).wait()
        if it == 0:
            pb_s[0, k, lo] = power[0, lo, piece(k, core), :] + pa_r[0, k, lo]
        else:
            for b in range(2):
                pb_s[1, k, b] = power[1, b, piece(k, core), :] + pa_r[1, k, b]
        pw(it, k, 1, lo).start()
        if it == 1:
            pw(it, k, 2, lo).start()
            pw(it, k, 4, lo).start()

    def pw_c(k):
        pw(0, k, 1, lo).wait()
        pc_s[0, k, lo] = pb_s[0, k, lo] + pb_r[0, k, lo]
        pw(0, k, 2, lo).start()

    def inverse(p):
        return 1.0 / jnp.sqrt(p / bins + small_eps)

    def pw_d(it, k):
        if it == 0:
            pw(it, k, 2, lo).wait_send()
            pw(it, k, 2, 1 - lo).wait_recv()
            pd_s[0, k, lo] = pc_s[0, k, lo]
            pd_s[0, k, 1 - lo] = pc_r[0, k, 1 - lo]
        else:
            for step in (1, 2, 4):
                pw(it, k, step, lo).wait()
            pd_s[1, k] = (pb_s[1, k] + pb_r[1, k]) + (pc_r[1, k] + pe_r[1, k])
        pw(it, k, 3, lo).start()
        for b in range(2):
            rinv[b, piece(k, core), :] = inverse(pd_s[it, k, b])

    def pw_e(it, k):
        pw(it, k, 3, lo).wait()
        for b in range(2):
            rinv[b, piece(k, core_o), :] = inverse(pd_r[it, k, b])

    for k in range(4):
        pw_a(0, k)
    for k in range(4):
        pw_b(0, k)
    for k in range(4):
        pw_c(k)
    for n in range(EARLY, AHEAD):
        x_copy(n // PIECES, n % PIECES).start()
    for k in range(4):
        pw_d(0, k)
    for k in range(4):
        pw_e(0, k)

    def grams(j, slices):
        real = imag = None
        for b in range(2):
            scored = []
            for i in range(2):
                parts = [(src[j, b, i, its, :] * rinv[b, its, :]).astype(bf16) for its in slices]
                scored.append(jnp.concatenate(parts, axis=0) if len(parts) > 1 else parts[0])
            pr, pi = scored
            br, bi = yb[j, b, 0], yb[j, b, 1]
            re = dot_nt(pr, br) + dot_nt(pi, bi)
            im = dot_nt(pi, br) - dot_nt(pr, bi)
            real, imag = (re, im) if b == 0 else (real + re, imag + im)
        return real, imag

    def triple(acc, m_hi, m_lo):
        n = acc.shape[0]
        both = jnp.concatenate([acc[:, :width], acc[:, width:]], axis=0)
        big = both.astype(bf16)
        small = (both - big.astype(f32)).astype(bf16)
        out = dot(big, m_hi[...]) + (dot(small, m_hi[...]) + dot(big, m_lo[...]))
        a, b = out[:n], out[n:]
        return a[:, :width] - b[:, width:], a[:, width:] + b[:, :width]

    def at(c):
        return pl.ds(pl.multiple_of(c * chunk, chunk), chunk)

    def at_own(c):
        return pl.ds(pl.multiple_of(y * half + c * chunk, chunk), chunk)

    def at_other(c):
        return pl.ds(pl.multiple_of((1 - y) * half + c * chunk, chunk), chunk)

    def s1a(j, c):
        return remote(gram.at[j, 1 - y, at(c)], r1.at[j, at(c)], s1a_send.at[j, c], s1a_recv.at[j, c], y_dev)

    def s2a(j, c, k):
        return remote(part.at[j, at(c)], r2a.at[j, c, k - 1], s2a_send.at[j, c], s2a_recv.at[j, c], peers[k - 1])

    def g(j, its_rows, c):
        ref = w_next.at[j, its_rows]
        return remote(ref, ref, g_send.at[j, c], g_recv.at[j, c], y_dev)

    def arrive(j):
        for p in range(PIECES):
            x_copy(j, p).wait_recv()
        xb[j] = xr[j].astype(bf16)
        yr, yi = times(w_hi[j, :, :width], w_hi[j, :, width:], xb[j, 0], xb[j, 1])
        keep(j, 1 - lo, yr, yi)
        for away in range(2):
            h = y if away else 1 - y
            real, imag = grams(j, [pl.ds(pl.multiple_of(h * half, half), half)])
            gram[j, h, :, :width] = real
            gram[j, h, :, width:] = imag
            if away == 0:
                for c in ORDER:
                    s1a(j, c).start()

    def sum1(j, t, c):
        s1a(j, c).wait_recv()
        part[j, at(c)] = gram[j, y, at(c)] + r1[j, at(c)]
        for k in range(1, high):
            s2a(j, c, k).start()
        u = j * CHUNKS + t
        for more in range(2):
            n = u + AHEAD + more
            turn = u >= CHUNKS if more else u <= CHUNKS
            due = jnp.logical_and(turn, n < nh * PIECES)
            pl.when(due)(lambda n=n: x_copy(n // PIECES, lax.rem(n, PIECES)).start())

    def update(j, t, c):
        many(r2a.at[j, c], s2a_recv.at[j, c]).wait()
        acc = part[j, at(c)]
        for k in range(high - 1):
            acc = acc + r2a[j, c, k]
        ar, ai = triple(acc * (1.0 / frames), w_hi.at[j], w_lo.at[j])
        w = flat[j, at_own(c)]
        wr, wi = w[:, :width], w[:, width:]
        w_next[j, at_own(c), :width] = wr + step_size * (wr - ar)
        w_next[j, at_own(c), width:] = wi + step_size * (wi - ai)
        g(j, at_own(c), c).start()

    def wx(j, from_lo):
        return remote(own.at[j, 1 - lo], w_out.at[from_lo * nh + j], wx_send.at[j], wx_recv.at[j], lo_dev)

    def w_home(j):
        return pltpu.make_async_copy(own.at[j, lo], w_out.at[lo * nh + j], home_sem.at[0, j])

    def p_home(j):
        return pltpu.make_async_copy(kept.at[j], p_out.at[lo * nh + j], home_sem.at[1, j])

    def mine(j):
        start = pl.multiple_of(y * half + hib * quarter, quarter)
        w = w_next[j, pl.ds(start, quarter), :]
        for l in range(2):
            for r in range(near):
                q = l * near + r
                if near == 1:
                    own[j, l] = w[q * rows:(q + 1) * rows]
                else:
                    pl.when(hir == r)(functools.partial(place, j, l, w[q * rows:(q + 1) * rows]))
        wx(j, lo).start()
        w_home(j).start()

    def place(j, l, w):
        own[j, l] = w

    def second(j, t, c):
        g(j, at_other(c), c).wait_recv()
        both = [at(c), pl.ds(pl.multiple_of(half + c * chunk, chunk), chunk)]
        w = jnp.concatenate([w_next[j, its] for its in both], axis=0)
        big = w.astype(bf16)
        small = (w - big.astype(f32)).astype(bf16)
        for h, its in enumerate(both):
            v_hi[j, its] = big[h * chunk:(h + 1) * chunk]
            v_lo[j, its] = small[h * chunk:(h + 1) * chunk]
        for b in range(2):
            x = (sig[lo * nh + j, 0], sig[lo * nh + j, 1]) if b == 0 else (xb[j, 0], xb[j, 1])
            yr, yi = times(big[:, :width], big[:, width:], *x)
            block = lo if b == 0 else 1 - lo
            squares = yr * yr + yi * yi
            for h, its in enumerate(both):
                here = slice(h * chunk, (h + 1) * chunk)
                src[j, block, 0, its] = yr[here]
                src[j, block, 1, its] = yi[here]
                yb[j, block, 0, its] = yr[here].astype(bf16)
                yb[j, block, 1, its] = yi[here].astype(bf16)
                power[1, block, its] += squares[here]

    units = nh * CHUNKS

    def stage_of(u):
        j, t = u // CHUNKS, lax.rem(u, CHUNKS)
        return j, t, lax.rem(t, 2) * 2 + t // 2

    def pipeline(s, carry):
        def on(lag, stage):
            u = s - lag
            pl.when(jnp.logical_and(u >= 0, u < units))(lambda: stage(*stage_of(u)))

        on(LAGS[0], sum1)
        on(LAGS[1], update)
        on(0, lambda j, t, c: pl.when(t == 0)(lambda: arrive(j)))
        on(LAGS[2], second)
        on(LAGS[2], lambda j, t, c: pl.when(t == CHUNKS - 1)(lambda: mine(j)))
        return carry

    lax.fori_loop(0, units, pipeline, 0)

    def run(stage, u):
        j, t = u // CHUNKS, u % CHUNKS
        stage(j, t, ORDER[t])

    for u in range(units - LAGS[0], units):
        run(sum1, u)
    tail = units - CHUNKS
    for u in range(units - LAGS[1], tail):
        run(update, u)
    for u in range(units - LAGS[2], tail):
        run(second, u)
        if u % CHUNKS == CHUNKS - 1:
            mine(u // CHUNKS)
    run(update, tail)
    run(update, tail + 1)
    run(second, tail)
    pw_a(1, 0)
    run(update, tail + 2)
    pw_b(1, 0)
    run(second, tail + 1)
    pw_a(1, 1)
    run(update, tail + 3)
    pw_b(1, 1)
    run(second, tail + 2)
    pw_a(1, 2)
    pw_d(1, 0)
    pw_b(1, 2)
    pw_e(1, 0)
    run(second, tail + 3)
    pw_a(1, 3)
    pw_d(1, 1)
    pw_b(1, 3)
    pw_e(1, 1)

    def dx(j, from_lo):
        return remote(prod.at[j], p_out.at[from_lo * nh + j], dx_send.at[j], dx_recv.at[j], lo_dev)

    lead = nh // 2

    def step_of(p):
        m = (p + nh - lead) // nh
        inner = lax.rem(m, 2)
        j = lo * lax.rem(p, nh) + (1 - lo) * (p - lead * inner - nh * (m // 2))
        return j, lo * (p // nh) + (1 - lo) * inner

    def s1b(j, l, i):
        return remote(
            gram_b.at[j, l, 0, i], r1b.at[j, l, i], s1b_send.at[j, l, i], s1b_recv.at[j, l, i], y_dev
        )

    def s2b(j, l, k):
        target = lax.rem(hi + k, high)
        i = 1 - lax.rem(target // near + hib, 2)
        return remote(
            last.at[j, l, i, lax.rem(target, near)], r2b.at[j, l, k - 1],
            s2b_send.at[j, l], s2b_recv.at[j, l], peers[k - 1],
        )

    def make_gram(p):
        j, l = step_of(p)
        slices = []
        for h in (1 - y, y):
            for sub in (1 - hib, hib):
                slices.append(pl.ds(pl.multiple_of(h * half + sub * quarter + l * eighth, eighth), eighth))
        real, imag = grams(j, slices)
        for h in range(2):
            for i in range(2):
                q = h * 2 + i
                gram_b[j, l, h, i, :, :width] = real[q * eighth:(q + 1) * eighth]
                gram_b[j, l, h, i, :, width:] = imag[q * eighth:(q + 1) * eighth]
        s1b(j, l, 0).start()
        s1b(j, l, 1).start()

    def sum1b(j, l, i):
        s1b(j, l, i).wait_recv()
        value = gram_b[j, l, 1, i] + r1b[j, l, i]
        for r in range(near):
            last[j, l, i, r] = value[r * rows:(r + 1) * rows]
        for k in range(1, high):
            there = lax.rem(lax.rem(hi + k, high) // near + hib, 2) == 1 - i
            pl.when(there)(lambda k=k: s2b(j, l, k).start())

    def send_on(p):
        j, l = step_of(p)
        sum1b(j, l, 0)

    def finish(p):
        j, l = step_of(p)
        sum1b(j, l, 1)
        many(r2b.at[j, l], s2b_recv.at[j, l]).wait()
        acc = last[j, l, 1, hir]
        for k in range(high - 1):
            acc = acc + r2b[j, l, k]
        ar, ai = triple(acc * (1.0 / frames), v_hi.at[j], v_lo.at[j])

        @pl.when(l != lo)
        def _():
            prod[j, :, :width] = ar
            prod[j, :, width:] = ai
            dx(j, lo).start()

        @pl.when(l == lo)
        def _():
            kept[j, :, :width] = ar
            kept[j, :, width:] = ai
            p_home(j).start()

    def each(stage, start, stop):
        def body(p, carry):
            stage(p)
            return carry

        lax.fori_loop(start, stop, body, 0)

    steps = 2 * nh
    each(make_gram, 0, lead)
    mine(nh - 1)
    pw_d(1, 2)
    pw_e(1, 2)
    each(send_on, 0, 1)
    pw_d(1, 3)
    pw_e(1, 3)
    each(make_gram, lead, steps)

    def both(p):
        pl.when(p < steps)(lambda: send_on(p))
        finish(p - BEHIND)

    def drain_first(j):
        for p in range(PIECES):
            x_copy(j, p).wait_send()
        for c in range(CHUNKS):
            s1a(j, c).wait_send()
            many(r2a.at[j, c], s2a_send.at[j, c]).wait()
            g(j, at_own(c), c).wait_send()
        w_home(j).wait()
        wx(j, lo).wait_send()
        wx(j, 1 - lo).wait_recv()

    def drain(j):
        for l in range(2):
            for i in range(2):
                s1b(j, l, i).wait_send()
            many(r2b.at[j, l], s2b_send.at[j, l]).wait()
        p_home(j).wait()
        dx(j, lo).wait_send()
        dx(j, 1 - lo).wait_recv()

    each(send_on, 1, BEHIND)
    each(drain_first, 0, nh)
    each(both, BEHIND, steps + BEHIND)

    each(drain, 0, nh)


def on_device(signal, demix):
    group = lax.axis_size("frame")
    bin_group = lax.axis_size("bin")
    nb, _, sensors, nt = signal.shape
    total, width2 = demix.shape[1:]
    rows = total // group
    high = group // 4
    half = total // 2
    eighth = total // 8
    nh = nb // 2
    out = jax.ShapeDtypeStruct((nb, rows, width2), f32)
    dma = pltpu.SemaphoreType.DMA
    hbm = pl.BlockSpec(memory_space=pl.ANY)
    piece = pltpu.VMEM((ITERS, 4, 2, eighth, nt), f32)
    own, product = pl.pallas_call(
        functools.partial(kernel, group, bin_group),
        out_shape=(out, out),
        in_specs=[hbm, hbm],
        out_specs=(hbm, hbm),
        scratch_shapes=[
            pltpu.VMEM((nb, 2, sensors, nt), bf16),
            pltpu.VMEM((nb, high, 2, 2, rows, width2), f32),
            pltpu.VMEM((nh, 2, sensors, nt), f32),
            pltpu.VMEM((nh, 2, sensors, nt), f32),
            pltpu.VMEM((nh, 2, sensors, nt), bf16),
            pltpu.VMEM((total, width2), f32),
            pltpu.VMEM((nh, total, width2), f32),
            pltpu.VMEM((nh, total, width2), f32),
            pltpu.VMEM((nh, total, width2), bf16),
            pltpu.VMEM((nh, total, width2), bf16),
            pltpu.VMEM((nh, total, width2), bf16),
            pltpu.VMEM((nh, total, width2), bf16),
            pltpu.VMEM((nh, 2, 2, total, nt), f32),
            pltpu.VMEM((nh, 2, 2, total, nt), bf16),
            pltpu.VMEM((nh, 2, half, width2), f32),
            pltpu.VMEM((nh, half, width2), f32),
            pltpu.VMEM((nh, half, width2), f32),
            pltpu.VMEM((nh, CHUNKS, high - 1, half // CHUNKS, width2), f32),
            pltpu.VMEM((nh, 2, 2, 2, eighth, width2), f32),
            pltpu.VMEM((nh, 2, 2, eighth, width2), f32),
            pltpu.VMEM((nh, 2, 2, high // 2, rows, width2), f32),
            pltpu.VMEM((nh, 2, high - 1, rows, width2), f32),
            pltpu.VMEM((nh, 2, rows, width2), f32),
            pltpu.VMEM((nh, rows, width2), f32),
            pltpu.VMEM((nh, rows, width2), f32),
            pltpu.VMEM((ITERS, 2, total, nt), f32),
            pltpu.VMEM((2, total, nt), f32),
            piece, piece, piece, piece, piece, piece, piece, piece,
            dma((nh, PIECES)), dma((nh, PIECES)),
            dma((ITERS, 4, 5)), dma((ITERS, 4, 5)),
            dma((nh, CHUNKS)), dma((nh, CHUNKS)),
            dma((nh, CHUNKS)), dma((nh, CHUNKS)),
            dma((nh, CHUNKS)), dma((nh, CHUNKS)),
            dma((nh, 2, 2)), dma((nh, 2, 2)),
            dma((nh, 2)), dma((nh, 2)),
            dma((nh,)), dma((nh,)),
            dma((nh,)), dma((nh,)),
            dma((nb,)), dma((nb,)), dma((2, nh)),
        ],
        compiler_params=pltpu.CompilerParams(
            collective_id=0, has_side_effects=True, vmem_limit_bytes=(51 if high == 2 else 62) * 1024 * 1024
        ),
    )(signal, demix.reshape(nb, high, 2, 2, rows, width2))
    direction = own - product
    return own + step_size * direction, direction


def solution(mesh):
    placed = (P("bin", None, None, "frame"), P("bin", None, None))
    return jax.shard_map(
        on_device,
        mesh=mesh,
        in_specs=placed,
        out_specs=(P("bin", "frame", None), P("bin", "frame", None)),
        check_vma=False,
    )
```

```python
import functools

import jax
import jax.numpy as jnp
from jax import lax
from jax.experimental import pallas as pl
from jax.experimental.pallas import tpu as pltpu
from jax.sharding import PartitionSpec as P

ITERS = 2
CHUNKS = 4
ORDER = (0, 2, 1, 3)
BEHIND = 2
LAGS = (1, 4, 7)
PIECES = 4
EARLY = 4
AHEAD = 9

step_size = 0.05
small_eps = 1e-06

MESH = pl.DeviceIdType.MESH
NT = (((1,), (1,)), ((), ()))
f32 = jnp.float32
bf16 = jnp.bfloat16


def dot(a, b):
    return jnp.dot(a, b, preferred_element_type=f32)


def dot_nt(a, b):
    return lax.dot_general(a, b, NT, preferred_element_type=f32)


def kernel(
    group, bin_group, sig_hbm, w_hbm, w_out, p_out,
    sig, w_in, xs, xr, xb, tmp, flat, w_next, w_hi, w_lo, v_hi, v_lo, src, yb,
    gram, r1, part, r2a, gram_b, r1b, last, r2b, own, prod, kept,
    power, rinv, pa_r, pb_s, pb_r, pc_s, pc_r, pd_s, pd_r, pe_r,
    x_send, x_recv, pw_send, pw_recv, s1a_send, s1a_recv, s2a_send, s2a_recv, g_send, g_recv,
    s1b_send, s1b_recv, s2b_send, s2b_recv, wx_send, wx_recv, dx_send, dx_recv, sig_sem, w_sem, home_sem,
):
    nb, high, _, _, rows, width2 = w_in.shape
    width = width2 // 2
    nt = sig.shape[3]
    nh = nb // 2
    total = 4 * high * rows
    half = total // 2
    quarter = total // 4
    eighth = total // 8
    chunk = half // CHUNKS
    frames = nt * group
    bins = nb * bin_group
    me = lax.axis_index("frame")
    mb = lax.axis_index("bin")
    y = lax.rem(me, 2)
    lo = lax.rem(me // 2, 2)
    hi = me // 4
    near = high // 2
    hib = hi // near
    hir = lax.rem(hi, near)
    core = lax.rem(mb, 2)
    core_o = 1 - core
    y_dev = {"frame": me + 1 - 2 * y}
    lo_dev = {"frame": me + 2 - 4 * lo}
    core_dev = {"bin": mb + 1 - 2 * core}
    x_dev = {"bin": lax.rem(mb + 2, bin_group)}
    both_dev = {"bin": lax.rem(mb + 2, bin_group), "frame": me + 2 - 4 * lo}
    peers = [{"frame": lax.rem(hi + k, high) * 4 + lax.rem(me, 4)} for k in range(1, high)]

    def remote(a, b, s, r, dev):
        return pltpu.make_async_remote_copy(
            src_ref=a, dst_ref=b, send_sem=s, recv_sem=r, device_id=dev, device_id_type=MESH
        )

    def many(ref, sem):
        return pltpu.make_async_copy(ref, ref, sem)

    def x_copy(j, p):
        deep = 2 * sig.shape[2] // PIECES
        ref = lambda a: a.at[j, p // 2, pl.ds(pl.multiple_of(lax.rem(p, 2) * deep, deep), deep)]
        return remote(ref(xs), ref(xr), x_send.at[j, p], x_recv.at[j, p], lo_dev)

    def load_sig(f):
        return pltpu.make_async_copy(sig_hbm.at[f], sig.at[f], sig_sem.at[f])

    def load_w(f):
        return pltpu.make_async_copy(w_hbm.at[f], w_in.at[f], w_sem.at[f])

    def widen(j):
        f = (1 - lo) * nh + j
        load_sig(f).wait()
        xs[j] = sig[f].astype(f32)

    for j in range(nh):
        load_sig((1 - lo) * nh + j).start()
    barrier = pltpu.get_barrier_semaphore()
    for dev in [y_dev, lo_dev, core_dev, x_dev, both_dev] + peers:
        pl.semaphore_signal(barrier, inc=1, device_id=dev, device_id_type=MESH)
    for j in range(nh):
        load_sig(lo * nh + j).start()
        load_w(lo * nh + j).start()
        load_w((1 - lo) * nh + j).start()
    power[...] = jnp.zeros_like(power)
    for j in range(nh):
        widen(j)
    pl.semaphore_wait(barrier, 5 + len(peers))
    for n in range(EARLY):
        x_copy(n // PIECES, n % PIECES).start()

    def permute(f, to):
        for yd in range(2):
            for hd in range(high):
                for ld in range(2):
                    q = yd * 2 * high + hd // near * 2 * near + ld * near + hd % near
                    to[q * rows:(q + 1) * rows, :] = w_in[f, hd, ld, yd]

    def times(wr, wi, xr_, xi_):
        return dot(wr, xr_) - dot(wi, xi_), dot(wr, xi_) + dot(wi, xr_)

    def keep(j, b, yr, yi):
        src[j, b, 0] = yr
        src[j, b, 1] = yi
        yb[j, b, 0] = yr.astype(bf16)
        yb[j, b, 1] = yi.astype(bf16)

    def split(j, w):
        big = w.astype(bf16)
        w_hi[j] = big
        w_lo[j] = (w - big.astype(f32)).astype(bf16)

    def first(j, carry):
        f = lo * nh + j
        load_sig(f).wait()
        load_w(f).wait()
        load_w((1 - lo) * nh + j).wait()
        permute(f, flat.at[j])
        split(j, flat[j])
        yr, yi = times(w_hi[j, :, :width], w_hi[j, :, width:], sig[f, 0], sig[f, 1])
        keep(j, lo, yr, yi)
        power[0, lo] += yr * yr + yi * yi
        f = (1 - lo) * nh + j
        permute(f, tmp)
        wr, wi = tmp[:, :width].astype(bf16), tmp[:, width:].astype(bf16)
        yr, yi = times(wr, wi, sig[f, 0], sig[f, 1])
        power[0, lo] += yr * yr + yi * yi
        return carry

    lax.fori_loop(0, nh, first, 0)

    def piece(k, who):
        return pl.ds(pl.multiple_of(who * half + ORDER[k] * chunk, chunk), chunk)

    def pw(it, k, step, block):
        sems = pw_send.at[it, k, step], pw_recv.at[it, k, step]
        if step == 0:
            if it == 0:
                return remote(power.at[0, block, piece(k, core_o)], pa_r.at[0, k, block], *sems, core_dev)
            return remote(power.at[1, :, piece(k, core_o)], pa_r.at[1, k], *sems, core_dev)
        if step == 3:
            return remote(pd_s.at[it, k], pd_r.at[it, k], *sems, core_dev)
        if it == 0:
            a, b, dev = (pb_s, pb_r, x_dev) if step == 1 else (pc_s, pc_r, lo_dev)
            return remote(a.at[0, k, block], b.at[0, k, block], *sems, dev)
        b, dev = {1: (pb_r, x_dev), 2: (pc_r, lo_dev), 4: (pe_r, both_dev)}[step]
        return remote(pb_s.at[1, k], b.at[1, k], *sems, dev)

    def pw_a(it, k):
        pw(it, k, 0, lo).start()

    def pw_b(it, k):
        pw(it, k, 0, lo).wait()
        if it == 0:
            pb_s[0, k, lo] = power[0, lo, piece(k, core), :] + pa_r[0, k, lo]
        else:
            for b in range(2):
                pb_s[1, k, b] = power[1, b, piece(k, core), :] + pa_r[1, k, b]
        pw(it, k, 1, lo).start()
        if it == 1:
            pw(it, k, 2, lo).start()
            pw(it, k, 4, lo).start()

    def pw_c(k):
        pw(0, k, 1, lo).wait()
        pc_s[0, k, lo] = pb_s[0, k, lo] + pb_r[0, k, lo]
        pw(0, k, 2, lo).start()

    def inverse(p):
        return 1.0 / jnp.sqrt(p / bins + small_eps)

    def pw_d(it, k):
        if it == 0:
            pw(it, k, 2, lo).wait_send()
            pw(it, k, 2, 1 - lo).wait_recv()
            pd_s[0, k, lo] = pc_s[0, k, lo]
            pd_s[0, k, 1 - lo] = pc_r[0, k, 1 - lo]
        else:
            for step in (1, 2, 4):
                pw(it, k, step, lo).wait()
            pd_s[1, k] = (pb_s[1, k] + pb_r[1, k]) + (pc_r[1, k] + pe_r[1, k])
        pw(it, k, 3, lo).start()
        for b in range(2):
            rinv[b, piece(k, core), :] = inverse(pd_s[it, k, b])

    def pw_e(it, k):
        pw(it, k, 3, lo).wait()
        for b in range(2):
            rinv[b, piece(k, core_o), :] = inverse(pd_r[it, k, b])

    for k in range(4):
        pw_a(0, k)
    for k in range(4):
        pw_b(0, k)
    for k in range(4):
        pw_c(k)
    for n in range(EARLY, AHEAD):
        x_copy(n // PIECES, n % PIECES).start()
    for k in range(4):
        pw_d(0, k)
    for k in range(4):
        pw_e(0, k)

    def grams(j, slices):
        real = imag = None
        for b in range(2):
            scored = []
            for i in range(2):
                parts = [(src[j, b, i, its, :] * rinv[b, its, :]).astype(bf16) for its in slices]
                scored.append(jnp.concatenate(parts, axis=0) if len(parts) > 1 else parts[0])
            pr, pi = scored
            br, bi = yb[j, b, 0], yb[j, b, 1]
            re = dot_nt(pr, br) + dot_nt(pi, bi)
            im = dot_nt(pi, br) - dot_nt(pr, bi)
            real, imag = (re, im) if b == 0 else (real + re, imag + im)
        return real, imag

    def triple(acc, m_hi, m_lo):
        n = acc.shape[0]
        both = jnp.concatenate([acc[:, :width], acc[:, width:]], axis=0)
        big = both.astype(bf16)
        small = (both - big.astype(f32)).astype(bf16)
        out = dot(big, m_hi[...]) + (dot(small, m_hi[...]) + dot(big, m_lo[...]))
        a, b = out[:n], out[n:]
        return a[:, :width] - b[:, width:], a[:, width:] + b[:, :width]

    def at(c):
        return pl.ds(pl.multiple_of(c * chunk, chunk), chunk)

    def at_own(c):
        return pl.ds(pl.multiple_of(y * half + c * chunk, chunk), chunk)

    def at_other(c):
        return pl.ds(pl.multiple_of((1 - y) * half + c * chunk, chunk), chunk)

    def s1a(j, c):
        return remote(gram.at[j, 1 - y, at(c)], r1.at[j, at(c)], s1a_send.at[j, c], s1a_recv.at[j, c], y_dev)

    def s2a(j, c, k):
        return remote(part.at[j, at(c)], r2a.at[j, c, k - 1], s2a_send.at[j, c], s2a_recv.at[j, c], peers[k - 1])

    def g(j, its_rows, c):
        ref = w_next.at[j, its_rows]
        return remote(ref, ref, g_send.at[j, c], g_recv.at[j, c], y_dev)

    def arrive(j):
        for p in range(PIECES):
            x_copy(j, p).wait_recv()
        xb[j] = xr[j].astype(bf16)
        yr, yi = times(w_hi[j, :, :width], w_hi[j, :, width:], xb[j, 0], xb[j, 1])
        keep(j, 1 - lo, yr, yi)
        for away in range(2):
            h = y if away else 1 - y
            real, imag = grams(j, [pl.ds(pl.multiple_of(h * half, half), half)])
            gram[j, h, :, :width] = real
            gram[j, h, :, width:] = imag
            if away == 0:
                for c in ORDER:
                    s1a(j, c).start()

    def sum1(j, t, c):
        s1a(j, c).wait_recv()
        part[j, at(c)] = gram[j, y, at(c)] + r1[j, at(c)]
        for k in range(1, high):
            s2a(j, c, k).start()
        n = j * CHUNKS + t + AHEAD
        pl.when(n < nh * PIECES)(lambda: x_copy(n // PIECES, lax.rem(n, PIECES)).start())

    def update(j, t, c):
        many(r2a.at[j, c], s2a_recv.at[j, c]).wait()
        acc = part[j, at(c)]
        for k in range(high - 1):
            acc = acc + r2a[j, c, k]
        ar, ai = triple(acc * (1.0 / frames), w_hi.at[j], w_lo.at[j])
        w = flat[j, at_own(c)]
        wr, wi = w[:, :width], w[:, width:]
        w_next[j, at_own(c), :width] = wr + step_size * (wr - ar)
        w_next[j, at_own(c), width:] = wi + step_size * (wi - ai)
        g(j, at_own(c), c).start()

    def wx(j, from_lo):
        return remote(own.at[j, 1 - lo], w_out.at[from_lo * nh + j], wx_send.at[j], wx_recv.at[j], lo_dev)

    def w_home(j):
        return pltpu.make_async_copy(own.at[j, lo], w_out.at[lo * nh + j], home_sem.at[0, j])

    def p_home(j):
        return pltpu.make_async_copy(kept.at[j], p_out.at[lo * nh + j], home_sem.at[1, j])

    def mine(j):
        start = pl.multiple_of(y * half + hib * quarter, quarter)
        w = w_next[j, pl.ds(start, quarter), :]
        for l in range(2):
            for r in range(near):
                q = l * near + r
                if near == 1:
                    own[j, l] = w[q * rows:(q + 1) * rows]
                else:
                    pl.when(hir == r)(functools.partial(place, j, l, w[q * rows:(q + 1) * rows]))
        wx(j, lo).start()
        w_home(j).start()

    def place(j, l, w):
        own[j, l] = w

    def second(j, t, c):
        g(j, at_other(c), c).wait_recv()
        both = [at(c), pl.ds(pl.multiple_of(half + c * chunk, chunk), chunk)]
        w = jnp.concatenate([w_next[j, its] for its in both], axis=0)
        big = w.astype(bf16)
        small = (w - big.astype(f32)).astype(bf16)
        for h, its in enumerate(both):
            v_hi[j, its] = big[h * chunk:(h + 1) * chunk]
            v_lo[j, its] = small[h * chunk:(h + 1) * chunk]
        for b in range(2):
            x = (sig[lo * nh + j, 0], sig[lo * nh + j, 1]) if b == 0 else (xb[j, 0], xb[j, 1])
            yr, yi = times(big[:, :width], big[:, width:], *x)
            block = lo if b == 0 else 1 - lo
            squares = yr * yr + yi * yi
            for h, its in enumerate(both):
                here = slice(h * chunk, (h + 1) * chunk)
                src[j, block, 0, its] = yr[here]
                src[j, block, 1, its] = yi[here]
                yb[j, block, 0, its] = yr[here].astype(bf16)
                yb[j, block, 1, its] = yi[here].astype(bf16)
                power[1, block, its] += squares[here]

    units = nh * CHUNKS

    def stage_of(u):
        j, t = u // CHUNKS, lax.rem(u, CHUNKS)
        return j, t, lax.rem(t, 2) * 2 + t // 2

    def pipeline(s, carry):
        def on(lag, stage):
            u = s - lag
            pl.when(jnp.logical_and(u >= 0, u < units))(lambda: stage(*stage_of(u)))

        on(LAGS[0], sum1)
        on(LAGS[1], update)
        on(0, lambda j, t, c: pl.when(t == 0)(lambda: arrive(j)))
        on(LAGS[2], second)
        on(LAGS[2], lambda j, t, c: pl.when(t == CHUNKS - 1)(lambda: mine(j)))
        return carry

    lax.fori_loop(0, units, pipeline, 0)

    def run(stage, u):
        j, t = u // CHUNKS, u % CHUNKS
        stage(j, t, ORDER[t])

    for u in range(units - LAGS[0], units):
        run(sum1, u)
    tail = units - CHUNKS
    for u in range(units - LAGS[1], tail):
        run(update, u)
    for u in range(units - LAGS[2], tail):
        run(second, u)
        if u % CHUNKS == CHUNKS - 1:
            mine(u // CHUNKS)
    run(update, tail)
    run(update, tail + 1)
    run(second, tail)
    pw_a(1, 0)
    run(update, tail + 2)
    pw_b(1, 0)
    run(second, tail + 1)
    pw_a(1, 1)
    run(update, tail + 3)
    pw_b(1, 1)
    run(second, tail + 2)
    pw_a(1, 2)
    pw_d(1, 0)
    pw_b(1, 2)
    pw_e(1, 0)
    run(second, tail + 3)
    pw_a(1, 3)
    pw_d(1, 1)
    pw_b(1, 3)
    pw_e(1, 1)

    def dx(j, from_lo):
        return remote(prod.at[j], p_out.at[from_lo * nh + j], dx_send.at[j], dx_recv.at[j], lo_dev)

    lead = nh // 2

    def step_of(p):
        m = (p + nh - lead) // nh
        inner = lax.rem(m, 2)
        j = lo * lax.rem(p, nh) + (1 - lo) * (p - lead * inner - nh * (m // 2))
        return j, lo * (p // nh) + (1 - lo) * inner

    def s1b(j, l, i):
        return remote(
            gram_b.at[j, l, 0, i], r1b.at[j, l, i], s1b_send.at[j, l, i], s1b_recv.at[j, l, i], y_dev
        )

    def s2b(j, l, k):
        target = lax.rem(hi + k, high)
        i = 1 - lax.rem(target // near + hib, 2)
        return remote(
            last.at[j, l, i, lax.rem(target, near)], r2b.at[j, l, k - 1],
            s2b_send.at[j, l], s2b_recv.at[j, l], peers[k - 1],
        )

    def make_gram(p):
        j, l = step_of(p)
        slices = []
        for h in (1 - y, y):
            for sub in (1 - hib, hib):
                slices.append(pl.ds(pl.multiple_of(h * half + sub * quarter + l * eighth, eighth), eighth))
        real, imag = grams(j, slices)
        for h in range(2):
            for i in range(2):
                q = h * 2 + i
                gram_b[j, l, h, i, :, :width] = real[q * eighth:(q + 1) * eighth]
                gram_b[j, l, h, i, :, width:] = imag[q * eighth:(q + 1) * eighth]
        s1b(j, l, 0).start()
        s1b(j, l, 1).start()

    def sum1b(j, l, i):
        s1b(j, l, i).wait_recv()
        value = gram_b[j, l, 1, i] + r1b[j, l, i]
        for r in range(near):
            last[j, l, i, r] = value[r * rows:(r + 1) * rows]
        for k in range(1, high):
            there = lax.rem(lax.rem(hi + k, high) // near + hib, 2) == 1 - i
            pl.when(there)(lambda k=k: s2b(j, l, k).start())

    def send_on(p):
        j, l = step_of(p)
        sum1b(j, l, 0)

    def finish(p):
        j, l = step_of(p)
        sum1b(j, l, 1)
        many(r2b.at[j, l], s2b_recv.at[j, l]).wait()
        acc = last[j, l, 1, hir]
        for k in range(high - 1):
            acc = acc + r2b[j, l, k]
        ar, ai = triple(acc * (1.0 / frames), v_hi.at[j], v_lo.at[j])

        @pl.when(l != lo)
        def _():
            prod[j, :, :width] = ar
            prod[j, :, width:] = ai
            dx(j, lo).start()

        @pl.when(l == lo)
        def _():
            kept[j, :, :width] = ar
            kept[j, :, width:] = ai
            p_home(j).start()

    def each(stage, start, stop):
        def body(p, carry):
            stage(p)
            return carry

        lax.fori_loop(start, stop, body, 0)

    steps = 2 * nh
    each(make_gram, 0, lead)
    mine(nh - 1)
    pw_d(1, 2)
    pw_e(1, 2)
    each(send_on, 0, 1)
    pw_d(1, 3)
    pw_e(1, 3)
    each(make_gram, lead, steps)

    def both(p):
        pl.when(p < steps)(lambda: send_on(p))
        finish(p - BEHIND)

    def drain_first(j):
        for p in range(PIECES):
            x_copy(j, p).wait_send()
        for c in range(CHUNKS):
            s1a(j, c).wait_send()
            many(r2a.at[j, c], s2a_send.at[j, c]).wait()
            g(j, at_own(c), c).wait_send()
        w_home(j).wait()
        wx(j, lo).wait_send()
        wx(j, 1 - lo).wait_recv()

    def drain(j):
        for l in range(2):
            for i in range(2):
                s1b(j, l, i).wait_send()
            many(r2b.at[j, l], s2b_send.at[j, l]).wait()
        p_home(j).wait()
        dx(j, lo).wait_send()
        dx(j, 1 - lo).wait_recv()

    each(send_on, 1, BEHIND)
    each(drain_first, 0, nh)
    each(both, BEHIND, steps + BEHIND)

    each(drain, 0, nh)


def on_device(signal, demix):
    group = lax.axis_size("frame")
    bin_group = lax.axis_size("bin")
    nb, _, sensors, nt = signal.shape
    total, width2 = demix.shape[1:]
    rows = total // group
    high = group // 4
    half = total // 2
    eighth = total // 8
    nh = nb // 2
    out = jax.ShapeDtypeStruct((nb, rows, width2), f32)
    dma = pltpu.SemaphoreType.DMA
    hbm = pl.BlockSpec(memory_space=pl.ANY)
    piece = pltpu.VMEM((ITERS, 4, 2, eighth, nt), f32)
    own, product = pl.pallas_call(
        functools.partial(kernel, group, bin_group),
        out_shape=(out, out),
        in_specs=[hbm, hbm],
        out_specs=(hbm, hbm),
        scratch_shapes=[
            pltpu.VMEM((nb, 2, sensors, nt), bf16),
            pltpu.VMEM((nb, high, 2, 2, rows, width2), f32),
            pltpu.VMEM((nh, 2, sensors, nt), f32),
            pltpu.VMEM((nh, 2, sensors, nt), f32),
            pltpu.VMEM((nh, 2, sensors, nt), bf16),
            pltpu.VMEM((total, width2), f32),
            pltpu.VMEM((nh, total, width2), f32),
            pltpu.VMEM((nh, total, width2), f32),
            pltpu.VMEM((nh, total, width2), bf16),
            pltpu.VMEM((nh, total, width2), bf16),
            pltpu.VMEM((nh, total, width2), bf16),
            pltpu.VMEM((nh, total, width2), bf16),
            pltpu.VMEM((nh, 2, 2, total, nt), f32),
            pltpu.VMEM((nh, 2, 2, total, nt), bf16),
            pltpu.VMEM((nh, 2, half, width2), f32),
            pltpu.VMEM((nh, half, width2), f32),
            pltpu.VMEM((nh, half, width2), f32),
            pltpu.VMEM((nh, CHUNKS, high - 1, half // CHUNKS, width2), f32),
            pltpu.VMEM((nh, 2, 2, 2, eighth, width2), f32),
            pltpu.VMEM((nh, 2, 2, eighth, width2), f32),
            pltpu.VMEM((nh, 2, 2, high // 2, rows, width2), f32),
            pltpu.VMEM((nh, 2, high - 1, rows, width2), f32),
            pltpu.VMEM((nh, 2, rows, width2), f32),
            pltpu.VMEM((nh, rows, width2), f32),
            pltpu.VMEM((nh, rows, width2), f32),
            pltpu.VMEM((ITERS, 2, total, nt), f32),
            pltpu.VMEM((2, total, nt), f32),
            piece, piece, piece, piece, piece, piece, piece, piece,
            dma((nh, PIECES)), dma((nh, PIECES)),
            dma((ITERS, 4, 5)), dma((ITERS, 4, 5)),
            dma((nh, CHUNKS)), dma((nh, CHUNKS)),
            dma((nh, CHUNKS)), dma((nh, CHUNKS)),
            dma((nh, CHUNKS)), dma((nh, CHUNKS)),
            dma((nh, 2, 2)), dma((nh, 2, 2)),
            dma((nh, 2)), dma((nh, 2)),
            dma((nh,)), dma((nh,)),
            dma((nh,)), dma((nh,)),
            dma((nb,)), dma((nb,)), dma((2, nh)),
        ],
        compiler_params=pltpu.CompilerParams(
            collective_id=0, has_side_effects=True, vmem_limit_bytes=(51 if high == 2 else 62) * 1024 * 1024
        ),
    )(signal, demix.reshape(nb, high, 2, 2, rows, width2))
    direction = own - product
    return own + step_size * direction, direction


def solution(mesh):
    placed = (P("bin", None, None, "frame"), P("bin", None, None))
    return jax.shard_map(
        on_device,
        mesh=mesh,
        in_specs=placed,
        out_specs=(P("bin", "frame", None), P("bin", "frame", None)),
        check_vma=False,
    )
```
